512 devices in a mesh: dp: 4 (over x), section: 8 (over y), tensor: 16 (over z, core).
Axes of the slice: x: 4, y: 8, z: 8, core: 2. Of those that a mesh axis runs over, the one named last changes fastest.
Arguments:
- arrivals: bfloat16 [8, 4, 128, 4096], P('section', 'dp', None, 'tensor'), may hold values from -30 to 30
- fresh: bfloat16 [2, 4, 128, 4096], P(None, 'dp', None, 'tensor'), may hold values from -30 to 30
- stash: bfloat16 [2, 8, 4, 128, 4096], P(None, 'section', 'dp', None, 'tensor'), may hold values from -30 to 30
- returning: bfloat16 [8, 4, 128, 4096], P('section', 'dp', None, 'tensor'), may hold values from -6 to 6
- loss_grad: bfloat16 [2, 4, 128, 4096], P(None, 'dp', None, 'tensor'), may hold values from -6 to 6
- gain: float32 [8, 4096], P('section', 'tensor'), may hold values from 0.1 to 1.9
- query_weight: bfloat16 [8, 4096, 4096], P('section', 'dp', 'tensor'), may hold values from -0.09375 to 0.09375
- key_weight: bfloat16 [8, 4096, 1024], P('section', 'dp', 'tensor'), may hold values from -0.09375 to 0.09375
- value_weight: bfloat16 [8, 4096, 1024], P('section', 'dp', 'tensor'), may hold values from -0.09375 to 0.09375
- w_out: bfloat16 [8, 4096, 4096], P('section', 'dp', 'tensor'), may hold values from -0.09375 to 0.09375
- plan: int32 [2, 4], replicated, may hold values from 0 to 3, each once within a row
- fresh_docs: int32 [2, 4, 128], replicated, may hold values from 0 to 5, never falling along the last dimension, each value on 1 to 64 neighbouring positions
- arrival_docs: int32 [8, 4, 128], P(None, 'dp'), may hold values from 0 to 5, never falling along the last dimension, each value on 1 to 64 neighbouring positions
- stash_docs: int32 [2, 8, 4, 128], P(None, 'section', 'dp'), may hold values from 0 to 5, never falling along the last dimension, each value on 1 to 64 neighbouring positions
Outputs:
- sent_forward: bfloat16 [8, 4, 128, 4096], P('section', 'dp', None, 'tensor')
- sent_backward: bfloat16 [8, 4, 128, 4096], P('section', 'dp', None, 'tensor')
- gain_grad: float32 [8, 4096], P('section', 'tensor')
The draws below stay inside these ranges and needn't reach their ends.
Inputs may be any that keep to these rules, and one draw needn't show every extreme that they name: Each row of plan names every packed row of its micro-batch once. `fresh_docs`: along a packed row document numbers never fall; every document holds 1 to 64 tokens and one holds exactly 64. `arrival_docs`: along a packed row document numbers never fall; every document holds 1 to 64 tokens and one holds exactly 64. `stash_docs`: along a packed row document numbers never fall; every document holds 1 to 64 tokens and one holds exactly 64.
All inputs are finite; a program needn't handle non-finite values.
Results may differ from the reference program's by a relative error of at most 0.035.
Values may be sent and summed in bfloat16 or wider, within the bound.
A program may use at most 64 MiB of HBM per device.

```python
import math
import jax
import jax.numpy as jnp
import numpy as np
from jax import lax

MODEL_WIDTH = 4096
QUERY_HEADS = 32
KEY_VALUE_HEADS = 8
HEAD_SIZE = 128
ROW_TOKENS = 128
TICKS = 2
DOCS = 6
DOC_MOST = 64
SECTION_LAYERS = 8
PACKS = 4
N_TENSOR = 16


def activation_rows(key, shape):
    key_base, key_row = jax.random.split(jax.random.fold_in(key, 11))
    column = jnp.arange(shape[-1], dtype=jnp.float32) / shape[-1]
    row_scale = 10.0 ** jax.random.uniform(key_row, shape[:-1] + (1,), minval=0.0, maxval=0.3)
    base = jnp.clip(jax.random.normal(key_base, shape), -5.0, 5.0)
    column_scale = 10.0 ** column
    values = 0.3 * base * row_scale * column_scale
    return values.astype(jnp.float32).astype(jnp.bfloat16)


def draw_arrivals(key, part):
    return activation_rows(jax.random.fold_in(key, 1), (SECTION_LAYERS, PACKS, ROW_TOKENS, MODEL_WIDTH))


def draw_fresh(key, part):
    return activation_rows(jax.random.fold_in(key, 2), (TICKS, PACKS, ROW_TOKENS, MODEL_WIDTH))


def draw_stash(key, part):
    return activation_rows(jax.random.fold_in(key, 3), (TICKS, SECTION_LAYERS, PACKS, ROW_TOKENS, MODEL_WIDTH))


def block_levels(rng, dims, shards, least, largest):
    factor_of = 1.0
    for position, blocks in shards:
        heights = jax.random.uniform(jax.random.fold_in(jax.random.fold_in(rng, 6), position), (blocks,), jnp.float32, least / len(shards), largest / len(shards))
        factor_of = factor_of * jnp.repeat(jnp.exp(heights), dims[position] // blocks).reshape((-1,) + (1,) * (len(dims) - 1 - position))
    return factor_of


def profile(number_of, total, limit, lean):
    portions = [(1 << 20) // math.isqrt(rank ** lean) + 1 for rank in range(2, number_of + 1)]
    spare, counts = total - limit - (number_of - 1), [1] * (number_of - 1)
    while spare > 0:
        candidates = [i for i in range(number_of - 1) if counts[i] < limit]
        whole, budget = sum([portions[i] for i in candidates]), spare
        for i in candidates:
            more = min(limit - counts[i], max(1, budget * portions[i] // whole), spare)
            counts[i] = counts[i] + more
            spare = spare - more
    return np.array([limit] + counts)


def uneven_parts(own_key, count, total, bound, skew):
    if count == 2:
        one = jax.random.randint(own_key, (), max(1, total - bound), min(bound, total - 1) + 1)
        return jnp.stack([one, total - one])
    tallies = jnp.asarray(profile(count, total, bound, skew), jnp.int32)
    twos = (count - 1) // 2
    source_of, sink = tallies[1:1 + 2 * twos:2], tallies[2:2 + 2 * twos:2]
    room = jnp.minimum(source_of - 1, bound - sink)
    shifted = jax.random.randint(jax.random.fold_in(own_key, 1), (twos,), 0, 1 << 20) % (room + 1)
    tallies = tallies.at[1:1 + 2 * twos:2].set(source_of - shifted).at[2:2 + 2 * twos:2].set(sink + shifted)
    return tallies[jax.random.permutation(jax.random.fold_in(own_key, 2), count)]


def bell_draw(rng, shape, scale, reach, cuts=(), kind=jnp.bfloat16):
    loudness = block_levels(rng, shape, cuts, -0.22, 0.18) if cuts else 1.0
    array = jax.random.normal(rng, shape, jnp.float32) * scale * loudness
    return jnp.minimum(jnp.maximum(array, -reach), reach).astype(kind)


def setup_inputs(seed: int = 0) -> dict:
    arg_keys = jax.random.split(jax.random.key(seed), 15)
    arrivals = draw_arrivals(jax.random.fold_in(arg_keys[14], 71), 0)
    fresh = draw_fresh(jax.random.fold_in(arg_keys[14], 71), 0)
    stash = draw_stash(jax.random.fold_in(arg_keys[14], 71), 0)
    returning = bell_draw(arg_keys[3], (SECTION_LAYERS, PACKS, ROW_TOKENS, MODEL_WIDTH), 1.0, 6.0, ((0, 8), (1, 4), (3, 16)))
    loss_grad = bell_draw(arg_keys[4], (TICKS, PACKS, ROW_TOKENS, MODEL_WIDTH), 1.0, 6.0, ((1, 4), (3, 16)))
    gain = jnp.clip(1.0 + 0.18 * jax.random.normal(arg_keys[5], (SECTION_LAYERS, MODEL_WIDTH), jnp.float32), 0.1, 1.9)
    query_weight = bell_draw(arg_keys[6], (SECTION_LAYERS, MODEL_WIDTH, QUERY_HEADS * HEAD_SIZE), MODEL_WIDTH ** -0.5, 0.09375, ((0, 8), (1, 4), (2, 16)))
    key_weight = bell_draw(arg_keys[7], (SECTION_LAYERS, MODEL_WIDTH, KEY_VALUE_HEADS * HEAD_SIZE), MODEL_WIDTH ** -0.5, 0.09375, ((0, 8), (1, 4), (2, 16)))
    value_weight = bell_draw(arg_keys[8], (SECTION_LAYERS, MODEL_WIDTH, KEY_VALUE_HEADS * HEAD_SIZE), MODEL_WIDTH ** -0.5, 0.09375, ((0, 8), (1, 4), (2, 16)))
    w_out = bell_draw(arg_keys[9], (SECTION_LAYERS, QUERY_HEADS * HEAD_SIZE, MODEL_WIDTH), (QUERY_HEADS * HEAD_SIZE) ** -0.5, 0.09375, ((0, 8), (1, 4), (2, 16)))
    plan = jax.vmap(lambda own: jax.random.permutation(own, PACKS))(jax.random.split(arg_keys[10], TICKS)).reshape((TICKS, PACKS)).astype(jnp.int32)
    fresh_docs = jax.vmap(lambda own: jnp.searchsorted(jnp.cumsum(uneven_parts(own, DOCS, ROW_TOKENS, DOC_MOST, 2)), jnp.arange(ROW_TOKENS), side="right"))(jax.random.split(arg_keys[11], TICKS * PACKS)).reshape((TICKS, PACKS, ROW_TOKENS)).astype(jnp.int32)
    arrival_docs = jax.vmap(lambda own: jnp.searchsorted(jnp.cumsum(uneven_parts(own, DOCS, ROW_TOKENS, DOC_MOST, 2)), jnp.arange(ROW_TOKENS), side="right"))(jax.random.split(arg_keys[12], SECTION_LAYERS * PACKS)).reshape((SECTION_LAYERS, PACKS, ROW_TOKENS)).astype(jnp.int32)
    stash_docs = jax.vmap(lambda own: jnp.searchsorted(jnp.cumsum(uneven_parts(own, DOCS, ROW_TOKENS, DOC_MOST, 2)), jnp.arange(ROW_TOKENS), side="right"))(jax.random.split(arg_keys[13], TICKS * SECTION_LAYERS * PACKS)).reshape((TICKS, SECTION_LAYERS, PACKS, ROW_TOKENS)).astype(jnp.int32)
    return dict(arrivals=arrivals, fresh=fresh, stash=stash, returning=returning, loss_grad=loss_grad, gain=gain, query_weight=query_weight, key_weight=key_weight, value_weight=value_weight, w_out=w_out, plan=plan, fresh_docs=fresh_docs, arrival_docs=arrival_docs, stash_docs=stash_docs)


norm_eps = 1e-05

def round_journey(values):
    return lax.optimization_barrier(values.astype(jnp.bfloat16)).astype(jnp.float32)

def normalize(hidden, gain_row):
    hidden_f = hidden.astype(jnp.float32)
    inverse = lax.rsqrt(lax.optimization_barrier(jnp.sum(hidden_f * hidden_f, axis=-1)) / MODEL_WIDTH + norm_eps)
    normed = (hidden_f * inverse[..., None] * gain_row).astype(jnp.bfloat16)
    return (hidden_f, inverse, normed)

def allowed_pairs(documents):
    same = documents[:, :, None] == documents[:, None, :]
    causal = jnp.arange(ROW_TOKENS)[:, None] >= jnp.arange(ROW_TOKENS)[None, :]
    return jnp.logical_and(same, causal[None])[:, None, None]

def attention_parts(normed, documents, query_weight, key_weight, value_weight):
    packed_rows = normed.shape[0]
    group_width = QUERY_HEADS // KEY_VALUE_HEADS
    flattened = normed.reshape(packed_rows * ROW_TOKENS, MODEL_WIDTH)
    query_rows = round_journey(jnp.dot(flattened, query_weight, preferred_element_type=jnp.float32)).reshape(packed_rows, ROW_TOKENS, KEY_VALUE_HEADS, group_width, HEAD_SIZE)
    heads_of_key = round_journey(jnp.dot(flattened, key_weight, preferred_element_type=jnp.float32)).reshape(packed_rows, ROW_TOKENS, KEY_VALUE_HEADS, HEAD_SIZE)
    heads_of_value = round_journey(jnp.dot(flattened, value_weight, preferred_element_type=jnp.float32)).reshape(packed_rows, ROW_TOKENS, KEY_VALUE_HEADS, HEAD_SIZE)
    scores = jnp.einsum('pikgd,pjkd->pkgij', query_rows, heads_of_key) * HEAD_SIZE ** (-0.5)
    raised = jnp.where(allowed_pairs(documents), jnp.exp(scores), 0.0)
    probs = raised / lax.optimization_barrier(jnp.sum(raised, axis=-1, keepdims=True))
    probs_half = round_journey(probs)
    return (query_rows, heads_of_key, heads_of_value, probs, probs_half)

def grouped_sum(left, right):
    left_groups = jnp.moveaxis(left, 1, 0)
    right_groups = jnp.moveaxis(right, 1, 0)

    def step(total, pair):
        part = jnp.dot(pair[0], pair[1].T, preferred_element_type=jnp.float32).astype(jnp.bfloat16)
        part = lax.optimization_barrier(part)
        return (total + part.astype(jnp.float32), None)
    start_total = jnp.zeros((left.shape[0], right.shape[0]), jnp.float32)
    total, unused_out = lax.scan(step, start_total, (left_groups, right_groups))
    return total

def forward_layer(hidden, documents, gain_row, query_weight, key_weight, value_weight, w_out):
    hidden_f, inverse, normed = normalize(hidden, gain_row)
    query_rows, heads_of_key, heads_of_value, probs, probs_half = attention_parts(normed, documents, query_weight, key_weight, value_weight)
    packed_rows = hidden.shape[0]
    mixed = jnp.einsum('pkgij,pjkd->pikgd', probs_half, heads_of_value).astype(jnp.bfloat16).reshape(packed_rows * ROW_TOKENS, QUERY_HEADS * HEAD_SIZE)
    update = jnp.dot(mixed, w_out, preferred_element_type=jnp.float32).reshape(packed_rows, ROW_TOKENS, MODEL_WIDTH)
    return (hidden_f + update).astype(jnp.bfloat16)

def backward_layer(hidden, documents, grad, gain_row, query_weight, key_weight, value_weight, w_out):
    hidden_f, inverse, normed = normalize(hidden, gain_row)
    query_rows, heads_of_key, heads_of_value, probs, probs_half = attention_parts(normed, documents, query_weight, key_weight, value_weight)
    packed_rows = hidden.shape[0]
    tokens = packed_rows * ROW_TOKENS
    group_width = QUERY_HEADS // KEY_VALUE_HEADS
    block = MODEL_WIDTH // N_TENSOR
    query_cols = QUERY_HEADS * HEAD_SIZE // N_TENSOR
    key_columns = KEY_VALUE_HEADS * HEAD_SIZE // N_TENSOR
    grad_flat = grad.reshape(tokens, MODEL_WIDTH)
    head_gradient = grouped_sum(grad_flat.reshape(tokens, N_TENSOR, block), w_out.reshape(QUERY_HEADS * HEAD_SIZE, N_TENSOR, block))
    head_gradient = round_journey(head_gradient).reshape(packed_rows, ROW_TOKENS, KEY_VALUE_HEADS, group_width, HEAD_SIZE)
    prob_grad = jnp.einsum('pikgd,pjkd->pkgij', head_gradient, heads_of_value)
    score_grad = round_journey(probs * (prob_grad - lax.optimization_barrier(jnp.sum(probs * prob_grad, axis=-1, keepdims=True))) * HEAD_SIZE ** (-0.5))
    query_grad = jnp.einsum('pkgij,pjkd->pikgd', score_grad, heads_of_key).astype(jnp.bfloat16).reshape(tokens, N_TENSOR, query_cols)
    key_grad = jnp.einsum('pkgij,pikgd->pjkd', score_grad, query_rows).astype(jnp.bfloat16).reshape(tokens, N_TENSOR, key_columns)
    value_grad = jnp.einsum('pkgij,pikgd->pjkd', probs_half, head_gradient).astype(jnp.bfloat16).reshape(tokens, N_TENSOR, key_columns)
    left = jnp.concatenate([query_grad, key_grad, value_grad], axis=-1)
    right = jnp.concatenate([query_weight.reshape(MODEL_WIDTH, N_TENSOR, query_cols), key_weight.reshape(MODEL_WIDTH, N_TENSOR, key_columns), value_weight.reshape(MODEL_WIDTH, N_TENSOR, key_columns)], axis=-1)
    normed_grad = grouped_sum(left, right)
    hidden_flat = hidden_f.reshape(tokens, MODEL_WIDTH)
    inverse_flat = inverse.reshape(tokens)
    scaled = normed_grad * gain_row
    row_dot = lax.optimization_barrier(jnp.sum(scaled * hidden_flat, axis=-1))
    result = grad_flat.astype(jnp.float32) + inverse_flat[:, None] * scaled - hidden_flat * (inverse_flat ** 3 * row_dot / MODEL_WIDTH)[:, None]
    gain_term = lax.optimization_barrier(jnp.sum(normed_grad * hidden_flat * inverse_flat[:, None], axis=0))
    return (result.astype(jnp.bfloat16).reshape(packed_rows, ROW_TOKENS, MODEL_WIDTH), gain_term)

def reference(arrivals, fresh, stash, returning, loss_grad, gain, query_weight, key_weight, value_weight, w_out, plan, fresh_docs, arrival_docs, stash_docs):
    layers = arrivals.shape[0]
    balanced = [fresh[tick][plan[tick]] for tick in range(TICKS)]
    balanced_docs = [fresh_docs[tick][plan[tick]] for tick in range(TICKS)]
    outgoing = [arrivals[section] for section in range(layers)]
    going_back = [returning[section] for section in range(layers)]
    gain_total = [jnp.zeros((MODEL_WIDTH,), jnp.float32) for section in range(layers)]
    for tick in range(TICKS):
        new_out = []
        new_back = []
        for section in range(layers):
            if section == 0:
                hidden = balanced[tick]
            else:
                hidden = outgoing[section - 1]
            if section > tick:
                documents = arrival_docs[section - tick - 1]
            else:
                documents = balanced_docs[tick - section]
            new_out.append(forward_layer(hidden, documents, gain[section], query_weight[section], key_weight[section], value_weight[section], w_out[section]))
            if section == layers - 1:
                grad = loss_grad[tick]
            else:
                grad = going_back[section + 1]
            back, term = backward_layer(stash[tick, section], stash_docs[tick, section], grad, gain[section], query_weight[section], key_weight[section], value_weight[section], w_out[section])
            new_back.append(back)
            gain_total[section] = gain_total[section] + term
        outgoing = new_out
        going_back = new_back
    gain_grad = jnp.stack(gain_total) / math.sqrt(TICKS * PACKS * ROW_TOKENS)
    return (jnp.stack(outgoing), jnp.stack(going_back), gain_grad)
```

```python
import math

import jax
import jax.numpy as jnp
from jax import lax
from jax.experimental import pallas as pl
from jax.experimental.pallas import tpu as pltpu
from jax.sharding import PartitionSpec as P

MODEL_WIDTH = 4096
HEAD = 128
TICKS = 2
ROWS = 128
BLK = 256
REPLICAS = 4
SECTIONS = 8
RING = 8
TENSOR = 16
SHARD = MODEL_WIDTH // REPLICAS
HALF = SHARD // 2
EPS = 1e-05
SCALE = HEAD ** (-0.5)
SEMS = 256
MESH = pl.DeviceIdType.MESH
F32 = jnp.float32
BF16 = jnp.bfloat16

S0, S1, F0, M0, F1, M1 = range(6)


def dot_nn(a, b):
    return lax.dot_general(a, b, (((1,), (0,)), ((), ())), preferred_element_type=F32)


def dot_nt(a, b):
    return lax.dot_general(a, b, (((1,), (1,)), ((), ())), preferred_element_type=F32)


def dot_tn(a, b):
    return lax.dot_general(a, b, (((0,), (0,)), ((), ())), preferred_element_type=F32)


def kernel(
    arrivals,
    fresh,
    stash,
    returning,
    loss_grad,
    gain,
    query_weight,
    key_weight,
    value_weight,
    w_out,
    plan,
    fresh_docs,
    arrival_docs,
    stash_docs,
    out_forward,
    out_backward,
    out_gain,
    wq,
    kv,
    ow,
    gath,
    gains,
    fr,
    yrecv,
    ysend,
    grad_in,
    masks,
    proj,
    proj_acc,
    inv_buf,
    part,
    part_sib,
    recv_sib,
    relay,
    relay_half,
    final,
    head_grad,
    grads,
    row_part,
    row_sib,
    row_all,
    gain_all,
    ss,
    rs,
    ls,
):
    d = lax.axis_index("dp")
    s = lax.axis_index("section")
    t = lax.axis_index("tensor")
    z = t // 2
    c = t % 2

    def zdev(k):
        return (d, s, lax.rem(t + 2 * k + TENSOR, TENSOR))

    sibling = (d, s, t + 1 - 2 * c)

    def xdev(k):
        return (lax.rem(d + k + REPLICAS, REPLICAS), s, t)

    def ydev(k):
        return (d, lax.rem(s + k + SECTIONS, SECTIONS), t)

    sends = []
    counter = [0]

    def new_id():
        counter[0] += 1
        return counter[0] - 1

    def describe(src, dst, i, device):
        return pltpu.make_async_remote_copy(
            src_ref=src,
            dst_ref=dst,
            send_sem=ss.at[i],
            recv_sem=rs.at[i],
            device_id=device,
            device_id_type=MESH,
        )

    def send(src, dst, device, keep=True):
        i = new_id()
        copy = describe(src, dst, i, device)
        copy.start()
        if keep:
            sends.append(copy)
            return i
        return (i, copy)

    def arrive(i, dst):
        describe(dst, dst, i, sibling).wait_recv()

    own = pl.ds(pl.multiple_of(d * SHARD, SHARD), SHARD)
    load_ow = pltpu.make_async_copy(w_out.at[0], ow.at[own], ls.at[0])
    load_wq = pltpu.make_async_copy(query_weight.at[0], wq.at[own], ls.at[1])
    load_ow.start()
    load_wq.start()
    kv[c, own, :] = jnp.concatenate([key_weight[0], value_weight[0]], axis=-1)

    peers = [zdev(k) for k in range(1, RING)] + [sibling]
    peers += [xdev(k) for k in range(1, REPLICAS)] + [ydev(1), ydev(-1)]
    barrier = pltpu.get_barrier_semaphore()
    for peer in peers:
        pl.semaphore_signal(barrier, inc=1, device_id=peer, device_id_type=MESH)
    pl.semaphore_wait(barrier, len(peers))

    def rows_of(k, half):
        base = lax.rem(d + k + REPLICAS, REPLICAS) * SHARD + half * HALF
        return pl.ds(pl.multiple_of(base, HALF), HALF)

    class Gather:
        def __init__(self, buffer, source):
            self.buffer = buffer
            self.source = source

        def start(self):
            b, src = self.buffer, self.source
            first, second = pl.ds(0, HALF), pl.ds(HALF, HALF)
            self.ids = [
                send(src.at[first], b.at[rows_of(0, 0)], xdev(1)),
                send(src.at[second], b.at[rows_of(0, 1)], xdev(-1)),
                send(src.at[second], b.at[rows_of(0, 1)], xdev(1)),
                send(src.at[first], b.at[rows_of(0, 0)], xdev(-1)),
            ]

        def forward(self):
            b = self.buffer
            arrive(self.ids[0], b.at[rows_of(-1, 0)])
            low = send(b.at[rows_of(-1, 0)], b.at[rows_of(-1, 0)], xdev(1))
            arrive(self.ids[1], b.at[rows_of(1, 1)])
            high = send(b.at[rows_of(1, 1)], b.at[rows_of(1, 1)], xdev(-1))
            self.ids += [low, high]

        def near(self):
            b = self.buffer
            arrive(self.ids[2], b.at[rows_of(-1, 1)])
            arrive(self.ids[3], b.at[rows_of(1, 0)])

        def far(self):
            b = self.buffer
            arrive(self.ids[4], b.at[rows_of(2, 0)])
            arrive(self.ids[5], b.at[rows_of(2, 1)])

    gather_ow = Gather(ow, w_out.at[0])
    gather_wq = Gather(wq, query_weight.at[0])
    gather_kv = Gather(kv.at[c], kv.at[c, own])

    gather_ow.start()

    y_forward = send(arrivals.at[0, 0], yrecv.at[0], ydev(1))
    y_backward = send(returning.at[0, 0], yrecv.at[1], ydev(-1))

    class AllGather:
        def __init__(self, buffer, half):
            self.b = buffer
            self.half = half

        def start(self):
            b = self.b
            src = b.at[c, 0]
            self.i3 = send(src, b.at[c, 3], zdev(2))
            self.i4 = send(src, b.at[c, 4], zdev(-2))
            self.i1 = send(src, b.at[c, 1], zdev(1))
            self.i2 = send(src, b.at[c, 2], zdev(-1))
            self.k0 = send(src, b.at[c, 0], sibling)

        def middle(self):
            b, h = self.b, self.half
            low, high = pl.ds(0, h), pl.ds(h, h)
            arrive(self.i3, b.at[c, 3])
            self.i5 = send(b.at[c, 3], b.at[c, 5], zdev(1))
            self.i7a = send(b.at[c, 3, low], b.at[c, 7, low], zdev(2))
            arrive(self.i4, b.at[c, 4])
            self.i6 = send(b.at[c, 4], b.at[c, 6], zdev(-1))
            self.i7b = send(b.at[c, 4, high], b.at[c, 7, high], zdev(-2))
            arrive(self.i1, b.at[c, 1])
            arrive(self.i2, b.at[c, 2])
            near = pl.ds(1, 4)
            self.k1 = send(b.at[c, near], b.at[c, near], sibling)

        def finish(self):
            b, h = self.b, self.half
            low, high = pl.ds(0, h), pl.ds(h, h)
            o = 1 - c
            arrive(self.i5, b.at[c, 5])
            arrive(self.i6, b.at[c, 6])
            arrive(self.i7a, b.at[c, 7, low])
            arrive(self.i7b, b.at[c, 7, high])
            away = pl.ds(5, 3)
            self.k2 = send(b.at[c, away], b.at[c, away], sibling)
            arrive(self.k0, b.at[o, 0])
            arrive(self.k1, b.at[o, pl.ds(1, 4)])

        def last(self):
            arrive(self.k2, self.b.at[1 - c, pl.ds(5, 3)])

    ag = [AllGather(gath.at[i], ROWS // 2) for i in range(6)]
    ag_gain = AllGather(gains, 8)

    gath[S0, c, 0] = stash[0, 0, 0]
    gath[S1, c, 0] = stash[1, 0, 0]
    gains[c, 0] = jnp.broadcast_to(gain[...], (16, BLK))
    ag_gain.start()
    ag[S0].start()
    ag[S1].start()

    fresh_ids = [[new_id() for _ in range(3)] for _ in range(TICKS)]

    @pl.when(s == 0)
    def _():
        for k in range(TICKS):
            fr[k, d] = fresh[k, 0]
            for n in range(3):
                describe(fresh.at[k, 0], fr.at[k, d], fresh_ids[k][n], xdev(n + 1)).start()

    def fresh_rows(k):
        for n in range(3):
            source = lax.rem(d - n - 1 + REPLICAS, REPLICAS)
            arrive(fresh_ids[k][n], fr.at[k, source])
        total = jnp.zeros((ROWS, BLK), BF16)
        for p in range(REPLICAS):
            total = jnp.where(plan[k, d] == p, fr[k, p], total)
        return total

    def balanced(k):
        total = jnp.zeros((1, ROWS), jnp.int32)
        for p in range(REPLICAS):
            total = jnp.where(plan[k, d] == p, fresh_docs[k, pl.ds(p, 1), :], total)
        return total

    causal = lax.broadcasted_iota(jnp.int32, (ROWS, ROWS), 0) >= lax.broadcasted_iota(
        jnp.int32, (ROWS, ROWS), 1
    )

    def store_mask(index, docs):
        across = jnp.broadcast_to(docs.astype(F32), (ROWS, ROWS))
        allowed = jnp.logical_and(across == across.T, causal)
        masks[index] = jnp.where(allowed, 1.0, 0.0)

    store_mask(0, stash_docs[0, 0])
    store_mask(1, stash_docs[1, 0])
    first_docs = balanced(0)
    for k in range(TICKS):
        arrived = arrival_docs[jnp.maximum(s - k - 1, 0)]
        new = first_docs if k == 0 else jnp.where(s == 0, balanced(1), first_docs)
        store_mask(2 + k, jnp.where(s > k, arrived, new))

    arrive(y_backward, yrecv.at[1])
    grad_in[0] = jnp.where(s == SECTIONS - 1, loss_grad[0, 0], yrecv[1])
    arrive(y_forward, yrecv.at[0])

    @pl.when(s == 0)
    def _():
        gath[F0, c, 0] = fresh_rows(0)

    @pl.when(s != 0)
    def _():
        gath[F0, c, 0] = yrecv[0]

    ag[F0].start()
    ag_gain.middle()
    ag[S0].middle()
    ag[S1].middle()

    def block_rows(p, core):
        k = (p + 1) // 2
        off = k * (1 - 2 * (p % 2))
        block = lax.rem(z + off + RING, RING) * 2 + core
        return pl.ds(pl.multiple_of(block * BLK, BLK), BLK)

    class ReduceScatter:
        def __init__(self, n, term):
            self.n = n
            self.term = term

        def fill(self, buffer, core, low, high):
            n, term = self.n, self.term

            def body(p, carry):
                buffer[n, p] = term(block_rows(p, core)).astype(BF16)
                return carry

            lax.fori_loop(low, high, body, 0)

        def start(self):
            n = self.n
            away, near = pl.ds(5, 3), pl.ds(0, 5)
            self.fill(part_sib, 1 - c, 5, 8)
            self.k1 = send(part_sib.at[n, away], recv_sib.at[n, away], sibling)
            self.fill(part_sib, 1 - c, 0, 5)
            self.k0 = send(part_sib.at[n, near], recv_sib.at[n, near], sibling)
            self.fill(part, c, 5, 8)
            arrive(self.k1, recv_sib.at[n, away])
            for p in range(5, 8):
                self.add(p)
            low, high = pl.ds(0, ROWS // 2), pl.ds(ROWS // 2, ROWS // 2)
            self.ra = send(part.at[n, 5], relay.at[n, 0], zdev(-1))
            self.rb = send(part.at[n, 6], relay.at[n, 1], zdev(1))
            self.ha = send(part.at[n, 7, low], relay_half.at[n, 0], zdev(-2))
            self.hb = send(part.at[n, 7, high], relay_half.at[n, 1], zdev(2))
            self.fill(part, c, 0, 5)
            arrive(self.k0, recv_sib.at[n, near])
            for p in (1, 2):
                self.add(p)
            self.d0 = send(part.at[n, 1], final.at[n, 0], zdev(-1))
            self.d1 = send(part.at[n, 2], final.at[n, 1], zdev(1))

        def add(self, p):
            n = self.n
            part[n, p] = (part[n, p].astype(F32) + recv_sib[n, p].astype(F32)).astype(BF16)

        def middle(self):
            n = self.n
            h = ROWS // 2
            arrive(self.ra, relay.at[n, 0])
            arrive(self.ha, relay_half.at[n, 0])
            sum3 = part[n, 3].astype(F32) + recv_sib[n, 3].astype(F32) + relay[n, 0].astype(F32)
            part[n, 3, pl.ds(0, h)] = (sum3[:h] + relay_half[n, 0].astype(F32)).astype(BF16)
            part[n, 3, pl.ds(h, h)] = sum3[h:].astype(BF16)
            self.d2 = send(part.at[n, 3], final.at[n, 2], zdev(-2))
            arrive(self.rb, relay.at[n, 1])
            arrive(self.hb, relay_half.at[n, 1])
            sum4 = part[n, 4].astype(F32) + recv_sib[n, 4].astype(F32) + relay[n, 1].astype(F32)
            part[n, 4, pl.ds(0, h)] = sum4[:h].astype(BF16)
            part[n, 4, pl.ds(h, h)] = (sum4[h:] + relay_half[n, 1].astype(F32)).astype(BF16)
            self.d3 = send(part.at[n, 4], final.at[n, 3], zdev(2))

        def finish(self):
            n = self.n
            total = part[n, 0].astype(F32) + recv_sib[n, 0].astype(F32)
            for q, i in enumerate((self.d0, self.d1, self.d2, self.d3)):
                arrive(i, final.at[n, q])
                total = total + final[n, q].astype(F32)
            return total

    def head_term(k):
        def term(rows):
            return dot_nt(grad_in[k], ow[rows, :])

        return term

    def weight_block(rows):
        return jnp.concatenate([wq[rows, :], kv[0, rows, :], kv[1, rows, :]], axis=1)

    def normed_term(k):
        def term(rows):
            return dot_nt(grads[k], weight_block(rows))

        return term

    gather_ow.forward()
    gather_wq.start()
    gather_kv.start()
    kv_own = send(kv.at[c, own], kv.at[c, own], sibling)
    load_ow.wait()
    load_wq.wait()
    ag[F0].middle()
    ag_gain.finish()
    ag[S0].finish()
    ag[S1].finish()
    ag[F0].finish()
    gather_ow.near()
    gather_ow.far()
    rs0 = ReduceScatter(0, head_term(0))
    rs0.start()
    gather_wq.forward()
    rs0.middle()
    gather_kv.forward()
    for index in (S0, S1, F0):
        ag[index].last()
    ag_gain.last()
    head_grad[0] = rs0.finish().astype(BF16)

    gather_kv.near()
    kv_ids = []
    for k in (-1, 1):
        rows = pl.ds(
            pl.multiple_of(lax.rem(d + k + REPLICAS, REPLICAS) * SHARD, SHARD), SHARD
        )
        kv_ids.append(send(kv.at[c, rows], kv.at[c, rows], sibling))
    gather_wq.near()
    gather_wq.far()
    gather_kv.far()
    rows = pl.ds(pl.multiple_of(lax.rem(d + 2, REPLICAS) * SHARD, SHARD), SHARD)
    kv_ids.append(send(kv.at[c, rows], kv.at[c, rows], sibling))
    arrive(kv_own, kv.at[1 - c, own])
    for i, k in zip(kv_ids, (-1, 1, 2)):
        rows = pl.ds(
            pl.multiple_of(lax.rem(d + k + REPLICAS, REPLICAS) * SHARD, SHARD), SHARD
        )
        arrive(i, kv.at[1 - c, rows])

    lane = lax.broadcasted_iota(jnp.int32, (ROWS, HEAD), 1)

    def project(indices, slots):
        count = len(indices)
        proj_acc[pl.ds(0, count * ROWS), :] = jnp.zeros((count * ROWS, 512), F32)

        def body(j, squares):
            p = j % RING
            core = j // RING
            g = gains[core, p, pl.ds(0, 1), :]
            pieces = []
            new = []
            for n, index in enumerate(indices):
                h = gath[index, core, p].astype(F32)
                sq = h * h
                new.append(squares[n] + sq[:, :HEAD] + sq[:, HEAD:])
                pieces.append((h * g).astype(BF16))
            lhs = pieces[0] if count == 1 else jnp.concatenate(pieces, axis=0)
            proj_acc[pl.ds(0, count * ROWS), :] += dot_nn(lhs, weight_block(block_rows(p, core)))
            return tuple(new)

        zero = jnp.zeros((ROWS, HEAD), F32)
        squares = lax.fori_loop(0, TENSOR, body, (zero,) * count)
        for n, slot in enumerate(slots):
            total = jnp.sum(squares[n], axis=-1, keepdims=True)
            inv = lax.rsqrt(total / MODEL_WIDTH + EPS)
            inv_buf[slot] = jnp.broadcast_to(inv, (ROWS, HEAD))
            acc = proj_acc[pl.ds(n * ROWS, ROWS), :] * inv
            low = acc[:, 256:384]
            high = acc[:, 384:512]
            key = jnp.where(lane < 64, low, pltpu.roll(high, 64, 1))
            value = jnp.where(lane < 64, pltpu.roll(low, 64, 1), high)
            proj[slot, 0] = acc[:, :128].astype(BF16)
            proj[slot, 1] = acc[:, 128:256].astype(BF16)
            proj[slot, 2] = key.astype(BF16)
            proj[slot, 3] = value.astype(BF16)

    def attention(slot, mask):
        q2 = jnp.concatenate([proj[slot, 0], proj[slot, 1]], axis=0)
        scores = dot_nt(q2, proj[slot, 2]) * SCALE
        allowed = jnp.concatenate([masks[mask], masks[mask]], axis=0) > 0.0
        raised = jnp.where(allowed, jnp.exp(scores), 0.0)
        return q2, raised / jnp.sum(raised, axis=-1, keepdims=True)

    def forward_attention(slot, mask, index):
        _, probs = attention(slot, mask)
        mixed = dot_nn(probs.astype(BF16), proj[slot, 3]).astype(BF16)
        gath[index, c, 0] = jnp.concatenate([mixed[:ROWS], mixed[ROWS:]], axis=1)

    def backward_attention(slot, mask, k):
        q2, probs = attention(slot, mask)
        key, value = proj[slot, 2], proj[slot, 3]
        hg = head_grad[k]
        hg2 = jnp.concatenate([hg[:, :HEAD], hg[:, HEAD:]], axis=0)
        prob_grad = dot_nt(hg2, value)
        inner = jnp.sum(probs * prob_grad, axis=-1, keepdims=True)
        score_grad = (probs * (prob_grad - inner) * SCALE).astype(BF16)
        query_grad = dot_nn(score_grad, key).astype(BF16).astype(F32)
        key_grad = dot_tn(score_grad, q2).astype(BF16).astype(F32)
        value_grad = dot_tn(probs.astype(BF16), hg2).astype(BF16).astype(F32)
        qf = q2.astype(F32)
        products = query_grad[:ROWS] * qf[:ROWS] + query_grad[ROWS:] * qf[ROWS:]
        products = products + key_grad * key.astype(F32) + value_grad * value.astype(F32)
        row = jnp.sum(products.T, axis=0, keepdims=True)
        row_part[k] = jnp.broadcast_to(row, (8, ROWS))
        low = jnp.where(lane < 64, key_grad, pltpu.roll(value_grad, 64, 1))
        high = jnp.where(lane < 64, pltpu.roll(key_grad, 64, 1), value_grad)
        grads[k] = jnp.concatenate(
            [query_grad[:ROWS], query_grad[ROWS:], low, high], axis=1
        ).astype(BF16)

    class RowSum:
        def __init__(self, k):
            self.k = k

        def start(self):
            self.i = send(row_part.at[self.k], row_sib.at[self.k], sibling)

        def middle(self):
            k = self.k
            arrive(self.i, row_sib.at[k])
            row_all[k, 0] = row_part[k] + row_sib[k]
            self.ids = [
                send(row_all.at[k, 0], row_all.at[k, n], zdev(n)) for n in range(1, RING)
            ]

        def finish(self):
            k = self.k
            total = row_all[k, 0]
            for n in range(1, RING):
                arrive(self.ids[n - 1], row_all.at[k, n])
                total = total + row_all[k, n]
            return jnp.broadcast_to(total[:1], (ROWS, ROWS)).T

    def backward_result(k, normed_grad, row):
        h = stash[k, 0, 0].astype(F32)
        inv = inv_buf[k][:, :1]
        scaled = normed_grad * gain[...]
        factor = inv * inv * row[:, :1] * (1.0 / MODEL_WIDTH)
        result = grad_in[k].astype(F32) + inv * scaled - h * factor
        term = jnp.sum(normed_grad * (h * inv), axis=0, keepdims=True)
        return result.astype(BF16), term

    def output_projection(index, hidden):
        def body(j, acc):
            p = j % RING
            core = j // RING
            return acc + dot_nn(gath[index, core, p], ow[block_rows(p, core), :])

        acc = lax.fori_loop(0, TENSOR, body, hidden.astype(F32))
        return acc.astype(BF16)

    project((S0, S1, F0), (0, 1, 2))
    backward_attention(0, 0, 0)
    rows0 = RowSum(0)
    rows0.start()
    rs1 = ReduceScatter(1, normed_term(0))
    rs1.start()
    rows0.middle()
    forward_attention(2, 2, M0)
    ag[M0].start()
    rs1.middle()
    ag[M0].middle()
    normed_grad = rs1.finish()
    result, gain_term0 = backward_result(0, normed_grad, rows0.finish())
    ysend[1] = result
    y_backward = send(ysend.at[1], yrecv.at[3], ydev(-1))
    ag[M0].finish()
    ag[M0].last()
    ysend[0] = output_projection(M0, gath[F0, c, 0])
    y_forward = send(ysend.at[0], yrecv.at[2], ydev(1))

    arrive(y_backward, yrecv.at[3])
    grad_in[1] = jnp.where(s == SECTIONS - 1, loss_grad[1, 0], yrecv[3])
    rs2 = ReduceScatter(2, head_term(1))
    rs2.start()
    arrive(y_forward, yrecv.at[2])

    @pl.when(s == 0)
    def _():
        gath[F1, c, 0] = fresh_rows(1)

    @pl.when(s != 0)
    def _():
        gath[F1, c, 0] = yrecv[2]

    ag[F1].start()
    rs2.middle()
    ag[F1].middle()
    head_grad[1] = rs2.finish().astype(BF16)
    backward_attention(1, 1, 1)
    rows1 = RowSum(1)
    rows1.start()
    rs3 = ReduceScatter(3, normed_term(1))
    rs3.start()
    rows1.middle()
    ag[F1].finish()
    ag[F1].last()
    project((F1,), (3,))
    forward_attention(3, 3, M1)
    ag[M1].start()
    rs3.middle()
    ag[M1].middle()
    normed_grad = rs3.finish()
    result, gain_term1 = backward_result(1, normed_grad, rows1.finish())
    out_backward[0, 0] = result
    gain_all[0] = jnp.broadcast_to(gain_term0 + gain_term1, (8, BLK))
    gain_ids = [send(gain_all.at[0], gain_all.at[n], xdev(n)) for n in range(1, REPLICAS)]
    ag[M1].finish()
    ag[M1].last()
    out_forward[0, 0] = output_projection(M1, gath[F1, c, 0])
    total = gain_all[0]
    for n in range(1, REPLICAS):
        arrive(gain_ids[n - 1], gain_all.at[n])
        total = total + gain_all[n]
    out_gain[...] = total[:1] * (1.0 / math.sqrt(TICKS * REPLICAS * ROWS))

    for copy in sends:
        copy.wait_send()

    @pl.when(s == 0)
    def _():
        for k in range(TICKS):
            for n in range(3):
                describe(fresh.at[k, 0], fr.at[k, d], fresh_ids[k][n], xdev(n + 1)).wait_send()


def local(*arguments):
    vmem = pl.BlockSpec(memory_space=pltpu.VMEM)
    anywhere = pl.BlockSpec(memory_space=pl.ANY)
    smem = pl.BlockSpec(memory_space=pltpu.SMEM)
    in_specs = [vmem] * 6 + [anywhere, vmem, vmem, anywhere, smem, vmem, vmem, vmem]
    block = (ROWS, BLK)
    scratch = [
        pltpu.VMEM((MODEL_WIDTH, BLK), BF16),
        pltpu.VMEM((2, MODEL_WIDTH, HEAD), BF16),
        pltpu.VMEM((MODEL_WIDTH, BLK), BF16),
        pltpu.VMEM((6, 2, RING) + block, BF16),
        pltpu.VMEM((2, RING, 16, BLK), F32),
        pltpu.VMEM((TICKS, REPLICAS) + block, BF16),
        pltpu.VMEM((4,) + block, BF16),
        pltpu.VMEM((2,) + block, BF16),
        pltpu.VMEM((TICKS,) + block, BF16),
        pltpu.VMEM((4, ROWS, ROWS), F32),
        pltpu.VMEM((4, 4, ROWS, HEAD), BF16),
        pltpu.VMEM((3 * ROWS, 512), F32),
        pltpu.VMEM((4, ROWS, HEAD), F32),
        pltpu.VMEM((4, RING) + block, BF16),
        pltpu.VMEM((4, RING) + block, BF16),
        pltpu.VMEM((4, RING) + block, BF16),
        pltpu.VMEM((4, 2) + block, BF16),
        pltpu.VMEM((4, 2, ROWS // 2, BLK), BF16),
        pltpu.VMEM((4, 4) + block, BF16),
        pltpu.VMEM((TICKS,) + block, BF16),
        pltpu.VMEM((TICKS, ROWS, 512), BF16),
        pltpu.VMEM((TICKS, 8, ROWS), F32),
        pltpu.VMEM((TICKS, 8, ROWS), F32),
        pltpu.VMEM((TICKS, RING, 8, ROWS), F32),
        pltpu.VMEM((REPLICAS, 8, BLK), F32),
        pltpu.SemaphoreType.DMA((SEMS,)),
        pltpu.SemaphoreType.DMA((SEMS,)),
        pltpu.SemaphoreType.DMA((2,)),
    ]
    return pl.pallas_call(
        kernel,
        out_shape=(
            jax.ShapeDtypeStruct((1, 1) + block, BF16),
            jax.ShapeDtypeStruct((1, 1) + block, BF16),
            jax.ShapeDtypeStruct((1, BLK), F32),
        ),
        in_specs=in_specs,
        out_specs=(vmem, vmem, vmem),
        scratch_shapes=scratch,
        compiler_params=pltpu.CompilerParams(
            collective_id=0, has_side_effects=True, vmem_limit_bytes=56 << 20
        ),
    )(*arguments)


def solution(mesh):
    return jax.shard_map(
        local,
        mesh=mesh,
        in_specs=(
            P("section", "dp", None, "tensor"),
            P(None, "dp", None, "tensor"),
            P(None, "section", "dp", None, "tensor"),
            P("section", "dp", None, "tensor"),
            P(None, "dp", None, "tensor"),
            P("section", "tensor"),
            P("section", "dp", "tensor"),
            P("section", "dp", "tensor"),
            P("section", "dp", "tensor"),
            P("section", "dp", "tensor"),
            P(),
            P(),
            P(None, "dp", None),
            P(None, "section", "dp", None),
        ),
        out_specs=(
            P("section", "dp", None, "tensor"),
            P("section", "dp", None, "tensor"),
            P("section", "tensor"),
        ),
        check_vma=False,
    )
```

```python
import math

import jax
import jax.numpy as jnp
from jax import lax
from jax.experimental import pallas as pl
from jax.experimental.pallas import tpu as pltpu
from jax.sharding import PartitionSpec as P

MODEL_WIDTH = 4096
HEAD = 128
TICKS = 2
ROWS = 128
BLK = 256
REPLICAS = 4
SECTIONS = 8
RING = 8
TENSOR = 16
SHARD = MODEL_WIDTH // REPLICAS
HALF = SHARD // 2
EPS = 1e-05
SCALE = HEAD ** (-0.5)
SEMS = 256
MESH = pl.DeviceIdType.MESH
F32 = jnp.float32
BF16 = jnp.bfloat16

S0, S1, F0, M0, F1, M1 = range(6)


def dot_nn(a, b):
    return lax.dot_general(a, b, (((1,), (0,)), ((), ())), preferred_element_type=F32)


def dot_nt(a, b):
    return lax.dot_general(a, b, (((1,), (1,)), ((), ())), preferred_element_type=F32)


def dot_tn(a, b):
    return lax.dot_general(a, b, (((0,), (0,)), ((), ())), preferred_element_type=F32)


def kernel(
    arrivals,
    fresh,
    stash,
    returning,
    loss_grad,
    gain,
    query_weight,
    key_weight,
    value_weight,
    w_out,
    plan,
    fresh_docs,
    arrival_docs,
    stash_docs,
    out_forward,
    out_backward,
    out_gain,
    wq,
    kv,
    ow,
    gath,
    gains,
    fr,
    yrecv,
    ysend,
    grad_in,
    masks,
    proj,
    proj_acc,
    inv_buf,
    part,
    part_sib,
    recv_sib,
    relay,
    relay_half,
    final,
    head_grad,
    grads,
    row_part,
    row_sib,
    row_all,
    gain_all,
    ss,
    rs,
    ls,
):
    d = lax.axis_index("dp")
    s = lax.axis_index("section")
    t = lax.axis_index("tensor")
    z = t // 2
    c = t % 2

    def zdev(k):
        return (d, s, lax.rem(t + 2 * k + TENSOR, TENSOR))

    sibling = (d, s, t + 1 - 2 * c)

    def xdev(k):
        return (lax.rem(d + k + REPLICAS, REPLICAS), s, t)

    def ydev(k):
        return (d, lax.rem(s + k + SECTIONS, SECTIONS), t)

    sends = []
    counter = [0]

    def new_id():
        counter[0] += 1
        return counter[0] - 1

    def describe(src, dst, i, device):
        return pltpu.make_async_remote_copy(
            src_ref=src,
            dst_ref=dst,
            send_sem=ss.at[i],
            recv_sem=rs.at[i],
            device_id=device,
            device_id_type=MESH,
        )

    def send(src, dst, device, keep=True):
        i = new_id()
        copy = describe(src, dst, i, device)
        copy.start()
        if keep:
            sends.append(copy)
            return i
        return (i, copy)

    def arrive(i, dst):
        describe(dst, dst, i, sibling).wait_recv()

    own = pl.ds(pl.multiple_of(d * SHARD, SHARD), SHARD)
    load_ow = pltpu.make_async_copy(w_out.at[0], ow.at[own], ls.at[0])
    load_wq = pltpu.make_async_copy(query_weight.at[0], wq.at[own], ls.at[1])
    load_key = pltpu.make_async_copy(key_weight.at[0], kv.at[c, d, pl.ds(0, 64)], ls.at[2])
    load_value = pltpu.make_async_copy(value_weight.at[0], kv.at[c, d, pl.ds(64, 64)], ls.at[3])
    for load in (load_key, load_value, load_wq, load_ow):
        load.start()

    peers = [zdev(k) for k in range(1, RING)] + [sibling]
    peers += [xdev(k) for k in range(1, REPLICAS)] + [ydev(1), ydev(-1)]
    barrier = pltpu.get_barrier_semaphore()
    for peer in peers:
        pl.semaphore_signal(barrier, inc=1, device_id=peer, device_id_type=MESH)
    pl.semaphore_wait(barrier, len(peers))

    def replica(k):
        return lax.rem(d + k + REPLICAS, REPLICAS)

    def rows_at(buffer):
        def at(k, half):
            base = replica(k) * SHARD + half * HALF
            return buffer.at[pl.ds(pl.multiple_of(base, HALF), HALF)]

        return at

    def kv_at(k, half):
        return kv.at[c, replica(k), pl.ds(half * 64, 64)]

    class Gather:
        def __init__(self, at, first, second):
            self.at = at
            self.first = first
            self.second = second

        def start(self):
            at = self.at
            self.ids = [
                send(self.first, at(0, 0), xdev(1)),
                send(self.second, at(0, 1), xdev(-1)),
                send(self.second, at(0, 1), xdev(1)),
                send(self.first, at(0, 0), xdev(-1)),
            ]

        def forward(self):
            at = self.at
            arrive(self.ids[0], at(-1, 0))
            low = send(at(-1, 0), at(-1, 0), xdev(1))
            arrive(self.ids[1], at(1, 1))
            high = send(at(1, 1), at(1, 1), xdev(-1))
            self.ids += [low, high]

        def near(self):
            arrive(self.ids[2], self.at(-1, 1))
            arrive(self.ids[3], self.at(1, 0))

        def far(self):
            arrive(self.ids[4], self.at(2, 0))
            arrive(self.ids[5], self.at(2, 1))

    first, second = pl.ds(0, HALF), pl.ds(HALF, HALF)
    gather_ow = Gather(rows_at(ow), w_out.at[0, first], w_out.at[0, second])
    gather_wq = Gather(rows_at(wq), query_weight.at[0, first], query_weight.at[0, second])
    gather_kv = Gather(kv_at, key_weight.at[0], value_weight.at[0])

    gather_ow.start()

    y_forward = send(arrivals.at[0, 0], yrecv.at[0], ydev(1))
    y_backward = send(returning.at[0, 0], yrecv.at[1], ydev(-1))

    class AllGather:
        def __init__(self, buffer, half):
            self.b = buffer
            self.half = half

        def start(self):
            b = self.b
            src = b.at[c, 0]
            self.i3 = send(src, b.at[c, 3], zdev(2))
            self.i4 = send(src, b.at[c, 4], zdev(-2))
            self.i1 = send(src, b.at[c, 1], zdev(1))
            self.i2 = send(src, b.at[c, 2], zdev(-1))
            self.k0 = send(src, b.at[c, 0], sibling)

        def middle(self):
            b, h = self.b, self.half
            low, high = pl.ds(0, h), pl.ds(h, h)
            arrive(self.i3, b.at[c, 3])
            self.i5 = send(b.at[c, 3], b.at[c, 5], zdev(1))
            self.i7a = send(b.at[c, 3, low], b.at[c, 7, low], zdev(2))
            arrive(self.i4, b.at[c, 4])
            self.i6 = send(b.at[c, 4], b.at[c, 6], zdev(-1))
            self.i7b = send(b.at[c, 4, high], b.at[c, 7, high], zdev(-2))
            arrive(self.i1, b.at[c, 1])
            arrive(self.i2, b.at[c, 2])
            near = pl.ds(1, 4)
            self.k1 = send(b.at[c, near], b.at[c, near], sibling)

        def finish(self):
            b, h = self.b, self.half
            low, high = pl.ds(0, h), pl.ds(h, h)
            o = 1 - c
            arrive(self.i5, b.at[c, 5])
            arrive(self.i6, b.at[c, 6])
            arrive(self.i7a, b.at[c, 7, low])
            arrive(self.i7b, b.at[c, 7, high])
            away = pl.ds(5, 3)
            self.k2 = send(b.at[c, away], b.at[c, away], sibling)
            arrive(self.k0, b.at[o, 0])
            arrive(self.k1, b.at[o, pl.ds(1, 4)])

        def last(self):
            arrive(self.k2, self.b.at[1 - c, pl.ds(5, 3)])

    ag = [AllGather(gath.at[i], ROWS // 2) for i in range(6)]
    ag_gain = AllGather(gains, 8)

    gath[S0, c, 0] = stash[0, 0, 0]
    gath[S1, c, 0] = stash[1, 0, 0]
    gains[c, 0] = jnp.broadcast_to(gain[...], (16, BLK))
    ag_gain.start()
    ag[S0].start()
    ag[S1].start()

    fresh_ids = [[new_id() for _ in range(3)] for _ in range(TICKS)]

    @pl.when(s == 0)
    def _():
        for k in range(TICKS):
            fr[k, d] = fresh[k, 0]
            for n in range(3):
                describe(fresh.at[k, 0], fr.at[k, d], fresh_ids[k][n], xdev(n + 1)).start()

    def fresh_rows(k):
        for n in range(3):
            source = lax.rem(d - n - 1 + REPLICAS, REPLICAS)
            arrive(fresh_ids[k][n], fr.at[k, source])
        total = jnp.zeros((ROWS, BLK), BF16)
        for p in range(REPLICAS):
            total = jnp.where(plan[k, d] == p, fr[k, p], total)
        return total

    def balanced(k):
        total = jnp.zeros((1, ROWS), jnp.int32)
        for p in range(REPLICAS):
            total = jnp.where(plan[k, d] == p, fresh_docs[k, pl.ds(p, 1), :], total)
        return total

    causal = lax.broadcasted_iota(jnp.int32, (ROWS, ROWS), 0) >= lax.broadcasted_iota(
        jnp.int32, (ROWS, ROWS), 1
    )

    def store_mask(index, docs):
        across = jnp.broadcast_to(docs.astype(F32), (ROWS, ROWS))
        allowed = jnp.logical_and(across == across.T, causal)
        masks[index] = jnp.where(allowed, 1.0, 0.0)

    store_mask(0, stash_docs[0, 0])
    store_mask(1, stash_docs[1, 0])
    first_docs = balanced(0)
    for k in range(TICKS):
        arrived = arrival_docs[jnp.maximum(s - k - 1, 0)]
        new = first_docs if k == 0 else jnp.where(s == 0, balanced(1), first_docs)
        store_mask(2 + k, jnp.where(s > k, arrived, new))

    arrive(y_backward, yrecv.at[1])
    grad_in[0] = jnp.where(s == SECTIONS - 1, loss_grad[0, 0], yrecv[1])
    arrive(y_forward, yrecv.at[0])

    @pl.when(s == 0)
    def _():
        gath[F0, c, 0] = fresh_rows(0)

    @pl.when(s != 0)
    def _():
        gath[F0, c, 0] = yrecv[0]

    ag[F0].start()
    ag_gain.middle()
    ag[S0].middle()
    ag[S1].middle()

    def block_of(p, core):
        k = (p + 1) // 2
        off = k * (1 - 2 * (p % 2))
        return lax.rem(z + off + RING, RING) * 2 + core

    def slot_of(block):
        off = lax.rem(block // 2 - z + RING, RING)
        return 2 * off + (off // 4) * (15 - 4 * off)

    def rows_of(block):
        return pl.ds(pl.multiple_of(block * BLK, BLK), BLK)

    class ReduceScatter:
        def __init__(self, n, term):
            self.n = n
            self.term = term

        def fill(self, buffer, core, low, high):
            n, term = self.n, self.term

            def body(p, carry):
                buffer[n, p] = term(block_of(p, core)).astype(BF16)
                return carry

            lax.fori_loop(low, high, body, 0, unroll=high - low)

        def start(self):
            n = self.n
            away, near = pl.ds(5, 3), pl.ds(0, 5)
            self.fill(part_sib, 1 - c, 5, 8)
            self.k1 = send(part_sib.at[n, away], recv_sib.at[n, away], sibling)
            self.fill(part_sib, 1 - c, 0, 5)
            self.k0 = send(part_sib.at[n, near], recv_sib.at[n, near], sibling)
            self.fill(part, c, 5, 8)
            arrive(self.k1, recv_sib.at[n, away])
            for p in range(5, 8):
                self.add(p)
            low, high = pl.ds(0, ROWS // 2), pl.ds(ROWS // 2, ROWS // 2)
            self.ra = send(part.at[n, 5], relay.at[n, 0], zdev(-1))
            self.rb = send(part.at[n, 6], relay.at[n, 1], zdev(1))
            self.ha = send(part.at[n, 7, low], relay_half.at[n, 0], zdev(-2))
            self.hb = send(part.at[n, 7, high], relay_half.at[n, 1], zdev(2))
            self.fill(part, c, 0, 5)
            arrive(self.k0, recv_sib.at[n, near])
            for p in (1, 2):
                self.add(p)
            self.d0 = send(part.at[n, 1], final.at[n, 0], zdev(-1))
            self.d1 = send(part.at[n, 2], final.at[n, 1], zdev(1))

        def add(self, p):
            n = self.n
            part[n, p] = (part[n, p].astype(F32) + recv_sib[n, p].astype(F32)).astype(BF16)

        def middle(self):
            n = self.n
            h = ROWS // 2
            arrive(self.ra, relay.at[n, 0])
            arrive(self.ha, relay_half.at[n, 0])
            sum3 = part[n, 3].astype(F32) + recv_sib[n, 3].astype(F32) + relay[n, 0].astype(F32)
            part[n, 3, pl.ds(0, h)] = (sum3[:h] + relay_half[n, 0].astype(F32)).astype(BF16)
            part[n, 3, pl.ds(h, h)] = sum3[h:].astype(BF16)
            self.d2 = send(part.at[n, 3], final.at[n, 2], zdev(-2))
            arrive(self.rb, relay.at[n, 1])
            arrive(self.hb, relay_half.at[n, 1])
            sum4 = part[n, 4].astype(F32) + recv_sib[n, 4].astype(F32) + relay[n, 1].astype(F32)
            part[n, 4, pl.ds(0, h)] = sum4[:h].astype(BF16)
            part[n, 4, pl.ds(h, h)] = (sum4[h:] + relay_half[n, 1].astype(F32)).astype(BF16)
            self.d3 = send(part.at[n, 4], final.at[n, 3], zdev(2))

        def finish(self):
            n = self.n
            total = part[n, 0].astype(F32) + recv_sib[n, 0].astype(F32)
            for q, i in enumerate((self.d0, self.d1, self.d2, self.d3)):
                arrive(i, final.at[n, q])
                total = total + final[n, q].astype(F32)
            return total

    def head_term(k):
        def term(block):
            return dot_nt(grad_in[k], ow[rows_of(block), :])

        return term

    def kv_block(block):
        lanes = pl.ds(pl.multiple_of(lax.rem(block, 4) * BLK, BLK), BLK)
        return jnp.concatenate([kv[0, block // 4, :, lanes], kv[1, block // 4, :, lanes]], axis=0)

    def normed_term(k):
        def term(block):
            query_part = dot_nt(grads[k, :, pl.ds(0, BLK)], wq[rows_of(block), :])
            return query_part + dot_nn(grads[k, :, pl.ds(BLK, BLK)], kv_block(block))

        return term

    gather_ow.forward()
    gather_wq.start()
    gather_kv.start()
    for load in (load_key, load_value, load_wq, load_ow):
        load.wait()
    kv_own = send(kv.at[c, d], kv.at[c, d], sibling)
    ag[F0].middle()
    ag_gain.finish()
    ag[S0].finish()
    ag[S1].finish()
    ag[F0].finish()
    gather_wq.forward()
    gather_ow.near()
    gather_ow.far()
    rs0 = ReduceScatter(0, head_term(0))
    rs0.start()
    gather_kv.forward()
    rs0.middle()
    for index in (S0, S1, F0):
        ag[index].last()
    ag_gain.last()
    head_grad[0] = rs0.finish().astype(BF16)

    lane = lax.broadcasted_iota(jnp.int32, (ROWS, HEAD), 1)

    class Project:
        def __init__(self, indices, slots):
            self.indices = indices
            self.slots = slots
            count = len(indices)
            self.rows = pl.ds(0, count * ROWS)
            proj_acc[self.rows, :] = jnp.zeros((count * ROWS, 512), F32)
            self.squares = (jnp.zeros((ROWS, HEAD), F32),) * count

        def add(self, owner):
            rows = self.rows
            squares = list(self.squares)
            columns = []
            for q in range(4):
                block = owner * 4 + q
                p, core = slot_of(block), q % 2
                g = gains[core, p, pl.ds(0, 1), :]
                pieces = []
                for n, index in enumerate(self.indices):
                    h = gath[index, core, p].astype(F32)
                    sq = h * h
                    squares[n] = squares[n] + sq[:, :HEAD] + sq[:, HEAD:]
                    pieces.append((h * g).astype(BF16))
                columns.append(jnp.concatenate(pieces, axis=0))
            self.squares = squares
            lhs = jnp.concatenate(columns, axis=1)
            weight = wq[pl.ds(pl.multiple_of(owner * SHARD, SHARD), SHARD), :]
            proj_acc[rows, pl.ds(0, BLK)] += dot_nn(lhs, weight)
            both = jnp.concatenate([kv[0, owner], kv[1, owner]], axis=0)
            proj_acc[rows, pl.ds(BLK, BLK)] += dot_nt(lhs, both)

        def done(self):
            for n, slot in enumerate(self.slots):
                total = jnp.sum(self.squares[n], axis=-1, keepdims=True)
                inv = lax.rsqrt(total / MODEL_WIDTH + EPS)
                inv_buf[slot] = jnp.broadcast_to(inv, (ROWS, HEAD))
                acc = proj_acc[pl.ds(n * ROWS, ROWS), :] * inv
                low = acc[:, 256:384]
                high = acc[:, 384:512]
                key = jnp.where(lane < 64, low, pltpu.roll(high, 64, 1))
                value = jnp.where(lane < 64, pltpu.roll(low, 64, 1), high)
                proj[slot, 0] = acc[:, :128].astype(BF16)
                proj[slot, 1] = acc[:, 128:256].astype(BF16)
                proj[slot, 2] = key.astype(BF16)
                proj[slot, 3] = value.astype(BF16)

    def attention(slot, mask):
        q2 = jnp.concatenate([proj[slot, 0], proj[slot, 1]], axis=0)
        scores = dot_nt(q2, proj[slot, 2]) * SCALE
        allowed = jnp.concatenate([masks[mask], masks[mask]], axis=0) > 0.0
        raised = jnp.where(allowed, jnp.exp(scores), 0.0)
        return q2, raised / jnp.sum(raised, axis=-1, keepdims=True)

    def forward_attention(slot, mask, index):
        _, probs = attention(slot, mask)
        mixed = dot_nn(probs.astype(BF16), proj[slot, 3]).astype(BF16)
        gath[index, c, 0] = jnp.concatenate([mixed[:ROWS], mixed[ROWS:]], axis=1)

    def backward_attention(slot, mask, k):
        q2, probs = attention(slot, mask)
        key, value = proj[slot, 2], proj[slot, 3]
        hg = head_grad[k]
        hg2 = jnp.concatenate([hg[:, :HEAD], hg[:, HEAD:]], axis=0)
        prob_grad = dot_nt(hg2, value)
        inner = jnp.sum(probs * prob_grad, axis=-1, keepdims=True)
        score_grad = (probs * (prob_grad - inner) * SCALE).astype(BF16)
        query_grad = dot_nn(score_grad, key).astype(BF16).astype(F32)
        key_grad = dot_tn(score_grad, q2).astype(BF16).astype(F32)
        value_grad = dot_tn(probs.astype(BF16), hg2).astype(BF16).astype(F32)
        qf = q2.astype(F32)
        products = query_grad[:ROWS] * qf[:ROWS] + query_grad[ROWS:] * qf[ROWS:]
        products = products + key_grad * key.astype(F32) + value_grad * value.astype(F32)
        row = jnp.sum(products.T, axis=0, keepdims=True)
        row_part[k] = jnp.broadcast_to(row, (8, ROWS))
        low = jnp.where(lane < 64, key_grad, pltpu.roll(value_grad, 64, 1))
        high = jnp.where(lane < 64, pltpu.roll(key_grad, 64, 1), value_grad)
        grads[k] = jnp.concatenate(
            [query_grad[:ROWS], query_grad[ROWS:], low, high], axis=1
        ).astype(BF16)

    class RowSum:
        def __init__(self, k):
            self.k = k

        def start(self):
            self.i = send(row_part.at[self.k], row_sib.at[self.k], sibling)

        def middle(self):
            k = self.k
            arrive(self.i, row_sib.at[k])
            row_all[k, 0] = row_part[k] + row_sib[k]
            self.ids = [
                send(row_all.at[k, 0], row_all.at[k, n], zdev(n)) for n in range(1, RING)
            ]

        def finish(self):
            k = self.k
            total = row_all[k, 0]
            for n in range(1, RING):
                arrive(self.ids[n - 1], row_all.at[k, n])
                total = total + row_all[k, n]
            return jnp.broadcast_to(total[:1], (ROWS, ROWS)).T

    def backward_result(k, normed_grad, row):
        h = stash[k, 0, 0].astype(F32)
        inv = inv_buf[k][:, :1]
        scaled = normed_grad * gain[...]
        factor = inv * inv * row[:, :1] * (1.0 / MODEL_WIDTH)
        result = grad_in[k].astype(F32) + inv * scaled - h * factor
        term = jnp.sum(normed_grad * (h * inv), axis=0, keepdims=True)
        return result.astype(BF16), term

    def output_projection(index, hidden):
        acc = hidden.astype(F32)
        for part_of in range(2):
            blocks = range(part_of * 8, part_of * 8 + 8)
            lhs = jnp.concatenate([gath[index, b % 2, slot_of(b)] for b in blocks], axis=1)
            acc = acc + dot_nn(lhs, ow[pl.ds(part_of * 8 * BLK, 8 * BLK), :])
        return acc.astype(BF16)

    project = Project((S0, S1, F0), (0, 1, 2))
    arrive(kv_own, kv.at[1 - c, d])
    project.add(replica(0))
    gather_kv.near()
    kv_ids = [send(kv.at[c, replica(k)], kv.at[c, replica(k)], sibling) for k in (-1, 1)]
    gather_wq.near()
    for i, k in zip(kv_ids, (-1, 1)):
        arrive(i, kv.at[1 - c, replica(k)])
    project.add(replica(-1))
    project.add(replica(1))
    gather_kv.far()
    kv_far = send(kv.at[c, replica(2)], kv.at[c, replica(2)], sibling)
    gather_wq.far()
    arrive(kv_far, kv.at[1 - c, replica(2)])
    project.add(replica(2))
    project.done()
    backward_attention(0, 0, 0)
    rows0 = RowSum(0)
    rows0.start()
    rs1 = ReduceScatter(1, normed_term(0))
    rs1.start()
    rows0.middle()
    forward_attention(2, 2, M0)
    ag[M0].start()
    rs1.middle()
    ag[M0].middle()
    normed_grad = rs1.finish()
    result, gain_term0 = backward_result(0, normed_grad, rows0.finish())
    ysend[1] = result
    y_backward = send(ysend.at[1], yrecv.at[3], ydev(-1))
    ag[M0].finish()
    ag[M0].last()
    ysend[0] = output_projection(M0, gath[F0, c, 0])
    y_forward = send(ysend.at[0], yrecv.at[2], ydev(1))

    arrive(y_backward, yrecv.at[3])
    grad_in[1] = jnp.where(s == SECTIONS - 1, loss_grad[1, 0], yrecv[3])
    rs2 = ReduceScatter(2, head_term(1))
    rs2.start()
    arrive(y_forward, yrecv.at[2])

    @pl.when(s == 0)
    def _():
        gath[F1, c, 0] = fresh_rows(1)

    @pl.when(s != 0)
    def _():
        gath[F1, c, 0] = yrecv[2]

    ag[F1].start()
    rs2.middle()
    ag[F1].middle()
    head_grad[1] = rs2.finish().astype(BF16)
    backward_attention(1, 1, 1)
    rows1 = RowSum(1)
    rows1.start()
    rs3 = ReduceScatter(3, normed_term(1))
    rs3.start()
    rows1.middle()
    ag[F1].finish()
    ag[F1].last()
    project = Project((F1,), (3,))
    for owner in range(REPLICAS):
        project.add(owner)
    project.done()
    forward_attention(3, 3, M1)
    ag[M1].start()
    rs3.middle()
    ag[M1].middle()
    normed_grad = rs3.finish()
    result, gain_term1 = backward_result(1, normed_grad, rows1.finish())
    out_backward[0, 0] = result
    gain_all[0] = jnp.broadcast_to(gain_term0 + gain_term1, (8, BLK))
    gain_ids = [send(gain_all.at[0], gain_all.at[n], xdev(n)) for n in range(1, REPLICAS)]
    ag[M1].finish()
    ag[M1].last()
    out_forward[0, 0] = output_projection(M1, gath[F1, c, 0])
    total = gain_all[0]
    for n in range(1, REPLICAS):
        arrive(gain_ids[n - 1], gain_all.at[n])
        total = total + gain_all[n]
    out_gain[...] = total[:1] * (1.0 / math.sqrt(TICKS * REPLICAS * ROWS))

    for copy in sends:
        copy.wait_send()

    @pl.when(s == 0)
    def _():
        for k in range(TICKS):
            for n in range(3):
                describe(fresh.at[k, 0], fr.at[k, d], fresh_ids[k][n], xdev(n + 1)).wait_send()


def local(*arguments):
    vmem = pl.BlockSpec(memory_space=pltpu.VMEM)
    anywhere = pl.BlockSpec(memory_space=pl.ANY)
    smem = pl.BlockSpec(memory_space=pltpu.SMEM)
    in_specs = [vmem] * 6 + [anywhere] * 4 + [smem, vmem, vmem, vmem]
    arguments = list(arguments)
    for n in (7, 8):
        arguments[n] = jnp.swapaxes(arguments[n], 1, 2)
    block = (ROWS, BLK)
    scratch = [
        pltpu.VMEM((MODEL_WIDTH, BLK), BF16),
        pltpu.VMEM((2, REPLICAS, HEAD, SHARD), BF16),
        pltpu.VMEM((MODEL_WIDTH, BLK), BF16),
        pltpu.VMEM((6, 2, RING) + block, BF16),
        pltpu.VMEM((2, RING, 16, BLK), F32),
        pltpu.VMEM((TICKS, REPLICAS) + block, BF16),
        pltpu.VMEM((4,) + block, BF16),
        pltpu.VMEM((2,) + block, BF16),
        pltpu.VMEM((TICKS,) + block, BF16),
        pltpu.VMEM((4, ROWS, ROWS), F32),
        pltpu.VMEM((4, 4, ROWS, HEAD), BF16),
        pltpu.VMEM((3 * ROWS, 512), F32),
        pltpu.VMEM((4, ROWS, HEAD), F32),
        pltpu.VMEM((4, RING) + block, BF16),
        pltpu.VMEM((4, RING) + block, BF16),
        pltpu.VMEM((4, RING) + block, BF16),
        pltpu.VMEM((4, 2) + block, BF16),
        pltpu.VMEM((4, 2, ROWS // 2, BLK), BF16),
        pltpu.VMEM((4, 4) + block, BF16),
        pltpu.VMEM((TICKS,) + block, BF16),
        pltpu.VMEM((TICKS, ROWS, 512), BF16),
        pltpu.VMEM((TICKS, 8, ROWS), F32),
        pltpu.VMEM((TICKS, 8, ROWS), F32),
        pltpu.VMEM((TICKS, RING, 8, ROWS), F32),
        pltpu.VMEM((REPLICAS, 8, BLK), F32),
        pltpu.SemaphoreType.DMA((SEMS,)),
        pltpu.SemaphoreType.DMA((SEMS,)),
        pltpu.SemaphoreType.DMA((4,)),
    ]
    return pl.pallas_call(
        kernel,
        out_shape=(
            jax.ShapeDtypeStruct((1, 1) + block, BF16),
            jax.ShapeDtypeStruct((1, 1) + block, BF16),
            jax.ShapeDtypeStruct((1, BLK), F32),
        ),
        in_specs=in_specs,
        out_specs=(vmem, vmem, vmem),
        scratch_shapes=scratch,
        compiler_params=pltpu.CompilerParams(
            collective_id=0, has_side_effects=True, vmem_limit_bytes=56 << 20
        ),
    )(*arguments)


def solution(mesh):
    return jax.shard_map(
        local,
        mesh=mesh,
        in_specs=(
            P("section", "dp", None, "tensor"),
            P(None, "dp", None, "tensor"),
            P(None, "section", "dp", None, "tensor"),
            P("section", "dp", None, "tensor"),
            P(None, "dp", None, "tensor"),
            P("section", "tensor"),
            P("section", "dp", "tensor"),
            P("section", "dp", "tensor"),
            P("section", "dp", "tensor"),
            P("section", "dp", "tensor"),
            P(),
            P(),
            P(None, "dp", None),
            P(None, "section", "dp", None),
        ),
        out_specs=(
            P("section", "dp", None, "tensor"),
            P("section", "dp", None, "tensor"),
            P("section", "tensor"),
        ),
        check_vma=False,
    )
```

```python
import math

import jax
import jax.numpy as jnp
from jax import lax
from jax.experimental import pallas as pl
from jax.experimental.pallas import tpu as pltpu
from jax.sharding import PartitionSpec as P

MODEL_WIDTH = 4096
HEAD = 128
TICKS = 2
ROWS = 128
BLK = 256
REPLICAS = 4
SECTIONS = 8
RING = 8
TENSOR = 16
SHARD = MODEL_WIDTH // REPLICAS
HALF = SHARD // 2
EPS = 1e-05
SCALE = HEAD ** (-0.5)
SEMS = 256
MESH = pl.DeviceIdType.MESH
F32 = jnp.float32
BF16 = jnp.bfloat16

S0, S1, F0, M0, F1, M1 = range(6)


def dot_nn(a, b):
    return lax.dot_general(a, b, (((1,), (0,)), ((), ())), preferred_element_type=F32)


def dot_nt(a, b):
    return lax.dot_general(a, b, (((1,), (1,)), ((), ())), preferred_element_type=F32)


def dot_tn(a, b):
    return lax.dot_general(a, b, (((0,), (0,)), ((), ())), preferred_element_type=F32)


def kernel(
    arrivals,
    fresh,
    stash,
    returning,
    loss_grad,
    gain,
    query_weight,
    key_weight,
    value_weight,
    w_out,
    plan,
    fresh_docs,
    arrival_docs,
    stash_docs,
    out_forward,
    out_backward,
    out_gain,
    wq,
    kv,
    ow,
    gath,
    gains,
    fr,
    yrecv,
    ysend,
    grad_in,
    masks,
    proj,
    proj_acc,
    inv_buf,
    part,
    part_sib,
    recv_sib,
    relay,
    relay_half,
    final,
    head_grad,
    grads,
    row_part,
    row_sib,
    row_all,
    gain_all,
    ss,
    rs,
    ls,
):
    d = lax.axis_index("dp")
    s = lax.axis_index("section")
    t = lax.axis_index("tensor")
    z = t // 2
    c = t % 2

    def zdev(k):
        return (d, s, lax.rem(t + 2 * k + TENSOR, TENSOR))

    sibling = (d, s, t + 1 - 2 * c)

    def xdev(k):
        return (lax.rem(d + k + REPLICAS, REPLICAS), s, t)

    def ydev(k):
        return (d, lax.rem(s + k + SECTIONS, SECTIONS), t)

    sends = []
    counter = [0]

    def new_id():
        counter[0] += 1
        return counter[0] - 1

    def describe(src, dst, i, device):
        return pltpu.make_async_remote_copy(
            src_ref=src,
            dst_ref=dst,
            send_sem=ss.at[i],
            recv_sem=rs.at[i],
            device_id=device,
            device_id_type=MESH,
        )

    def send(src, dst, device, keep=True):
        i = new_id()
        copy = describe(src, dst, i, device)
        copy.start()
        if keep:
            sends.append(copy)
            return i
        return (i, copy)

    def arrive(i, dst):
        describe(dst, dst, i, sibling).wait_recv()

    own = pl.ds(pl.multiple_of(d * SHARD, SHARD), SHARD)
    load_ow = pltpu.make_async_copy(w_out.at[0], ow.at[own], ls.at[0])
    load_wq = pltpu.make_async_copy(query_weight.at[0], wq.at[own], ls.at[1])
    load_key = pltpu.make_async_copy(key_weight.at[0], kv.at[c, d, pl.ds(0, 64)], ls.at[2])
    load_value = pltpu.make_async_copy(value_weight.at[0], kv.at[c, d, pl.ds(64, 64)], ls.at[3])
    for load in (load_key, load_value, load_wq, load_ow):
        load.start()

    peers = [zdev(k) for k in range(1, RING)] + [sibling]
    peers += [xdev(k) for k in range(1, REPLICAS)] + [ydev(1), ydev(-1)]
    barrier = pltpu.get_barrier_semaphore()
    for peer in peers:
        pl.semaphore_signal(barrier, inc=1, device_id=peer, device_id_type=MESH)
    pl.semaphore_wait(barrier, len(peers))

    def replica(k):
        return lax.rem(d + k + REPLICAS, REPLICAS)

    def rows_at(buffer):
        def at(k, half):
            base = replica(k) * SHARD + half * HALF
            return buffer.at[pl.ds(pl.multiple_of(base, HALF), HALF)]

        return at

    def kv_at(k, half):
        return kv.at[c, replica(k), pl.ds(half * 64, 64)]

    class Gather:
        def __init__(self, at, first, second):
            self.at = at
            self.first = first
            self.second = second

        def start(self):
            at = self.at
            self.ids = [
                send(self.first, at(0, 0), xdev(1)),
                send(self.second, at(0, 1), xdev(-1)),
                send(self.second, at(0, 1), xdev(1)),
                send(self.first, at(0, 0), xdev(-1)),
            ]

        def forward(self):
            at = self.at
            arrive(self.ids[0], at(-1, 0))
            low = send(at(-1, 0), at(-1, 0), xdev(1))
            arrive(self.ids[1], at(1, 1))
            high = send(at(1, 1), at(1, 1), xdev(-1))
            self.ids += [low, high]

        def near(self):
            arrive(self.ids[2], self.at(-1, 1))
            arrive(self.ids[3], self.at(1, 0))

        def far(self):
            arrive(self.ids[4], self.at(2, 0))
            arrive(self.ids[5], self.at(2, 1))

    first, second = pl.ds(0, HALF), pl.ds(HALF, HALF)
    gather_ow = Gather(rows_at(ow), w_out.at[0, first], w_out.at[0, second])
    gather_wq = Gather(rows_at(wq), query_weight.at[0, first], query_weight.at[0, second])
    gather_kv = Gather(kv_at, key_weight.at[0], value_weight.at[0])

    gather_ow.start()

    y_forward = send(arrivals.at[0, 0], yrecv.at[0], ydev(1))
    y_backward = send(returning.at[0, 0], yrecv.at[1], ydev(-1))

    class AllGather:
        def __init__(self, buffer, half):
            self.b = buffer
            self.half = half

        def start(self):
            b = self.b
            src = b.at[c, 0]
            self.i3 = send(src, b.at[c, 3], zdev(2))
            self.i4 = send(src, b.at[c, 4], zdev(-2))
            self.i1 = send(src, b.at[c, 1], zdev(1))
            self.i2 = send(src, b.at[c, 2], zdev(-1))
            self.k0 = send(src, b.at[c, 0], sibling)

        def middle(self):
            b, h = self.b, self.half
            low, high = pl.ds(0, h), pl.ds(h, h)
            arrive(self.i3, b.at[c, 3])
            self.i5 = send(b.at[c, 3], b.at[c, 5], zdev(1))
            self.i7a = send(b.at[c, 3, low], b.at[c, 7, low], zdev(2))
            arrive(self.i4, b.at[c, 4])
            self.i6 = send(b.at[c, 4], b.at[c, 6], zdev(-1))
            self.i7b = send(b.at[c, 4, high], b.at[c, 7, high], zdev(-2))
            arrive(self.i1, b.at[c, 1])
            arrive(self.i2, b.at[c, 2])
            near = pl.ds(1, 4)
            self.k1 = send(b.at[c, near], b.at[c, near], sibling)

        def finish(self):
            b, h = self.b, self.half
            low, high = pl.ds(0, h), pl.ds(h, h)
            o = 1 - c
            arrive(self.i5, b.at[c, 5])
            arrive(self.i6, b.at[c, 6])
            arrive(self.i7a, b.at[c, 7, low])
            arrive(self.i7b, b.at[c, 7, high])
            away = pl.ds(5, 3)
            self.k2 = send(b.at[c, away], b.at[c, away], sibling)
            arrive(self.k0, b.at[o, 0])
            arrive(self.k1, b.at[o, pl.ds(1, 4)])

        def last(self):
            arrive(self.k2, self.b.at[1 - c, pl.ds(5, 3)])

    ag = [AllGather(gath.at[i], ROWS // 2) for i in range(6)]
    ag_gain = AllGather(gains, 8)

    gath[S0, c, 0] = stash[0, 0, 0]
    gath[S1, c, 0] = stash[1, 0, 0]
    gains[c, 0] = jnp.broadcast_to(gain[...], (16, BLK))
    ag_gain.start()
    ag[S0].start()
    ag[S1].start()

    fresh_ids = [[new_id() for _ in range(3)] for _ in range(TICKS)]

    @pl.when(s == 0)
    def _():
        for k in range(TICKS):
            fr[k, d] = fresh[k, 0]
            for n in range(3):
                describe(fresh.at[k, 0], fr.at[k, d], fresh_ids[k][n], xdev(n + 1)).start()

    def fresh_rows(k):
        for n in range(3):
            source = lax.rem(d - n - 1 + REPLICAS, REPLICAS)
            arrive(fresh_ids[k][n], fr.at[k, source])
        total = jnp.zeros((ROWS, BLK), BF16)
        for p in range(REPLICAS):
            total = jnp.where(plan[k, d] == p, fr[k, p], total)
        return total

    def balanced(k):
        total = jnp.zeros((1, ROWS), jnp.int32)
        for p in range(REPLICAS):
            total = jnp.where(plan[k, d] == p, fresh_docs[k, pl.ds(p, 1), :], total)
        return total

    causal = lax.broadcasted_iota(jnp.int32, (ROWS, ROWS), 0) >= lax.broadcasted_iota(
        jnp.int32, (ROWS, ROWS), 1
    )

    def store_mask(index, docs):
        across = jnp.broadcast_to(docs.astype(F32), (ROWS, ROWS))
        allowed = jnp.logical_and(across == across.T, causal)
        masks[index] = jnp.where(allowed, 1.0, 0.0)

    store_mask(0, stash_docs[0, 0])
    store_mask(1, stash_docs[1, 0])
    first_docs = balanced(0)
    for k in range(TICKS):
        arrived = arrival_docs[jnp.maximum(s - k - 1, 0)]
        new = first_docs if k == 0 else jnp.where(s == 0, balanced(1), first_docs)
        store_mask(2 + k, jnp.where(s > k, arrived, new))

    arrive(y_backward, yrecv.at[1])
    grad_in[0] = jnp.where(s == SECTIONS - 1, loss_grad[0, 0], yrecv[1])
    arrive(y_forward, yrecv.at[0])

    @pl.when(s == 0)
    def _():
        gath[F0, c, 0] = fresh_rows(0)

    @pl.when(s != 0)
    def _():
        gath[F0, c, 0] = yrecv[0]

    ag[F0].start()
    ag_gain.middle()
    ag[S0].middle()
    ag[S1].middle()

    def block_of(p, core):
        k = (p + 1) // 2
        off = k * (1 - 2 * (p % 2))
        return lax.rem(z + off + RING, RING) * 2 + core

    def slot_of(block):
        off = lax.rem(block // 2 - z + RING, RING)
        return 2 * off + (off // 4) * (15 - 4 * off)

    def rows_of(block):
        return pl.ds(pl.multiple_of(block * BLK, BLK), BLK)

    class ReduceScatter:
        def __init__(self, n, term):
            self.n = n
            self.term = term

        def fill(self, buffer, core, low, high):
            n, term = self.n, self.term

            def body(p, carry):
                buffer[n, p] = term(block_of(p, core)).astype(BF16)
                return carry

            lax.fori_loop(low, high, body, 0, unroll=high - low)

        def start(self):
            n = self.n
            away, near = pl.ds(5, 3), pl.ds(0, 5)
            self.fill(part_sib, 1 - c, 5, 8)
            self.k1 = send(part_sib.at[n, away], recv_sib.at[n, away], sibling)
            self.fill(part_sib, 1 - c, 0, 5)
            self.k0 = send(part_sib.at[n, near], recv_sib.at[n, near], sibling)
            self.fill(part, c, 5, 8)
            arrive(self.k1, recv_sib.at[n, away])
            for p in range(5, 8):
                self.add(p)
            low, high = pl.ds(0, ROWS // 2), pl.ds(ROWS // 2, ROWS // 2)
            self.ra = send(part.at[n, 5], relay.at[n, 0], zdev(-1))
            self.rb = send(part.at[n, 6], relay.at[n, 1], zdev(1))
            self.ha = send(part.at[n, 7, low], relay_half.at[n, 0], zdev(-2))
            self.hb = send(part.at[n, 7, high], relay_half.at[n, 1], zdev(2))
            self.fill(part, c, 0, 5)
            arrive(self.k0, recv_sib.at[n, near])
            for p in (1, 2):
                self.add(p)
            self.d0 = send(part.at[n, 1], final.at[n, 0], zdev(-1))
            self.d1 = send(part.at[n, 2], final.at[n, 1], zdev(1))

        def add(self, p):
            n = self.n
            part[n, p] = (part[n, p].astype(F32) + recv_sib[n, p].astype(F32)).astype(BF16)

        def middle(self):
            n = self.n
            h = ROWS // 2
            arrive(self.ra, relay.at[n, 0])
            arrive(self.ha, relay_half.at[n, 0])
            sum3 = part[n, 3].astype(F32) + recv_sib[n, 3].astype(F32) + relay[n, 0].astype(F32)
            part[n, 3, pl.ds(0, h)] = (sum3[:h] + relay_half[n, 0].astype(F32)).astype(BF16)
            part[n, 3, pl.ds(h, h)] = sum3[h:].astype(BF16)
            self.d2 = send(part.at[n, 3], final.at[n, 2], zdev(-2))
            arrive(self.rb, relay.at[n, 1])
            arrive(self.hb, relay_half.at[n, 1])
            sum4 = part[n, 4].astype(F32) + recv_sib[n, 4].astype(F32) + relay[n, 1].astype(F32)
            part[n, 4, pl.ds(0, h)] = sum4[:h].astype(BF16)
            part[n, 4, pl.ds(h, h)] = (sum4[h:] + relay_half[n, 1].astype(F32)).astype(BF16)
            self.d3 = send(part.at[n, 4], final.at[n, 3], zdev(2))

        def finish(self):
            n = self.n
            total = part[n, 0].astype(F32) + recv_sib[n, 0].astype(F32)
            for q, i in enumerate((self.d0, self.d1, self.d2, self.d3)):
                arrive(i, final.at[n, q])
                total = total + final[n, q].astype(F32)
            return total

    def head_term(k):
        def term(block):
            return dot_nt(grad_in[k], ow[rows_of(block), :])

        return term

    def kv_block(block):
        lanes = pl.ds(pl.multiple_of(lax.rem(block, 4) * BLK, BLK), BLK)
        return jnp.concatenate([kv[0, block // 4, :, lanes], kv[1, block // 4, :, lanes]], axis=0)

    def normed_term(k):
        def term(block):
            query_part = dot_nt(grads[k, :, pl.ds(0, BLK)], wq[rows_of(block), :])
            return query_part + dot_nn(grads[k, :, pl.ds(BLK, BLK)], kv_block(block))

        return term

    gather_ow.forward()
    gather_wq.start()
    for load in (load_key, load_value, load_wq, load_ow):
        load.wait()
    kv_own = send(kv.at[c, d], kv.at[c, d], sibling)
    ag[F0].middle()
    ag_gain.finish()
    ag[S0].finish()
    ag[S1].finish()
    ag[F0].finish()
    gather_ow.near()
    gather_kv.start()
    gather_wq.forward()
    gather_ow.far()
    rs0 = ReduceScatter(0, head_term(0))
    rs0.start()
    gather_kv.forward()
    rs0.middle()
    for index in (S0, S1, F0):
        ag[index].last()
    ag_gain.last()
    head_grad[0] = rs0.finish().astype(BF16)

    lane = lax.broadcasted_iota(jnp.int32, (ROWS, HEAD), 1)

    class Project:
        def __init__(self, indices, slots):
            self.indices = indices
            self.slots = slots
            count = len(indices)
            self.rows = pl.ds(0, count * ROWS)
            proj_acc[self.rows, :] = jnp.zeros((count * ROWS, 512), F32)
            self.squares = (jnp.zeros((ROWS, HEAD), F32),) * count

        def add(self, owner):
            rows = self.rows
            squares = list(self.squares)
            columns = []
            for q in range(4):
                block = owner * 4 + q
                p, core = slot_of(block), q % 2
                g = gains[core, p, pl.ds(0, 1), :]
                pieces = []
                for n, index in enumerate(self.indices):
                    h = gath[index, core, p].astype(F32)
                    sq = h * h
                    squares[n] = squares[n] + sq[:, :HEAD] + sq[:, HEAD:]
                    pieces.append((h * g).astype(BF16))
                columns.append(jnp.concatenate(pieces, axis=0))
            self.squares = squares
            lhs = jnp.concatenate(columns, axis=1)
            weight = wq[pl.ds(pl.multiple_of(owner * SHARD, SHARD), SHARD), :]
            proj_acc[rows, pl.ds(0, BLK)] += dot_nn(lhs, weight)
            both = jnp.concatenate([kv[0, owner], kv[1, owner]], axis=0)
            proj_acc[rows, pl.ds(BLK, BLK)] += dot_nt(lhs, both)

        def done(self):
            for n, slot in enumerate(self.slots):
                total = jnp.sum(self.squares[n], axis=-1, keepdims=True)
                inv = lax.rsqrt(total / MODEL_WIDTH + EPS)
                inv_buf[slot] = jnp.broadcast_to(inv, (ROWS, HEAD))
                acc = proj_acc[pl.ds(n * ROWS, ROWS), :] * inv
                low = acc[:, 256:384]
                high = acc[:, 384:512]
                key = jnp.where(lane < 64, low, pltpu.roll(high, 64, 1))
                value = jnp.where(lane < 64, pltpu.roll(low, 64, 1), high)
                proj[slot, 0] = acc[:, :128].astype(BF16)
                proj[slot, 1] = acc[:, 128:256].astype(BF16)
                proj[slot, 2] = key.astype(BF16)
                proj[slot, 3] = value.astype(BF16)

    def attention(slot, mask):
        q2 = jnp.concatenate([proj[slot, 0], proj[slot, 1]], axis=0)
        scores = dot_nt(q2, proj[slot, 2]) * SCALE
        allowed = jnp.concatenate([masks[mask], masks[mask]], axis=0) > 0.0
        raised = jnp.where(allowed, jnp.exp(scores), 0.0)
        return q2, raised / jnp.sum(raised, axis=-1, keepdims=True)

    def forward_attention(slot, mask, index):
        _, probs = attention(slot, mask)
        mixed = dot_nn(probs.astype(BF16), proj[slot, 3]).astype(BF16)
        gath[index, c, 0] = jnp.concatenate([mixed[:ROWS], mixed[ROWS:]], axis=1)

    def backward_attention(slot, mask, k):
        q2, probs = attention(slot, mask)
        key, value = proj[slot, 2], proj[slot, 3]
        hg = head_grad[k]
        hg2 = jnp.concatenate([hg[:, :HEAD], hg[:, HEAD:]], axis=0)
        prob_grad = dot_nt(hg2, value)
        inner = jnp.sum(probs * prob_grad, axis=-1, keepdims=True)
        score_grad = (probs * (prob_grad - inner) * SCALE).astype(BF16)
        query_grad = dot_nn(score_grad, key).astype(BF16).astype(F32)
        key_grad = dot_tn(score_grad, q2).astype(BF16).astype(F32)
        value_grad = dot_tn(probs.astype(BF16), hg2).astype(BF16).astype(F32)
        qf = q2.astype(F32)
        products = query_grad[:ROWS] * qf[:ROWS] + query_grad[ROWS:] * qf[ROWS:]
        products = products + key_grad * key.astype(F32) + value_grad * value.astype(F32)
        row = jnp.sum(products.T, axis=0, keepdims=True)
        row_part[k] = jnp.broadcast_to(row, (8, ROWS))
        low = jnp.where(lane < 64, key_grad, pltpu.roll(value_grad, 64, 1))
        high = jnp.where(lane < 64, pltpu.roll(key_grad, 64, 1), value_grad)
        grads[k] = jnp.concatenate(
            [query_grad[:ROWS], query_grad[ROWS:], low, high], axis=1
        ).astype(BF16)

    class RowSum:
        def __init__(self, k):
            self.k = k

        def start(self):
            self.i = send(row_part.at[self.k], row_sib.at[self.k], sibling)

        def middle(self):
            k = self.k
            arrive(self.i, row_sib.at[k])
            row_all[k, 0] = row_part[k] + row_sib[k]
            self.ids = [
                send(row_all.at[k, 0], row_all.at[k, n], zdev(n)) for n in range(1, RING)
            ]

        def finish(self):
            k = self.k
            total = row_all[k, 0]
            for n in range(1, RING):
                arrive(self.ids[n - 1], row_all.at[k, n])
                total = total + row_all[k, n]
            return jnp.broadcast_to(total[:1], (ROWS, ROWS)).T

    def backward_result(k, normed_grad, row):
        h = stash[k, 0, 0].astype(F32)
        inv = inv_buf[k][:, :1]
        scaled = normed_grad * gain[...]
        factor = inv * inv * row[:, :1] * (1.0 / MODEL_WIDTH)
        result = grad_in[k].astype(F32) + inv * scaled - h * factor
        term = jnp.sum(normed_grad * (h * inv), axis=0, keepdims=True)
        return result.astype(BF16), term

    def output_projection(index, hidden):
        acc = hidden.astype(F32)
        for part_of in range(2):
            blocks = range(part_of * 8, part_of * 8 + 8)
            lhs = jnp.concatenate([gath[index, b % 2, slot_of(b)] for b in blocks], axis=1)
            acc = acc + dot_nn(lhs, ow[pl.ds(part_of * 8 * BLK, 8 * BLK), :])
        return acc.astype(BF16)

    project = Project((S0, S1, F0), (0, 1, 2))
    arrive(kv_own, kv.at[1 - c, d])
    project.add(replica(0))
    gather_kv.near()
    kv_ids = [send(kv.at[c, replica(k)], kv.at[c, replica(k)], sibling) for k in (-1, 1)]
    gather_wq.near()
    for i, k in zip(kv_ids, (-1, 1)):
        arrive(i, kv.at[1 - c, replica(k)])
    project.add(replica(-1))
    project.add(replica(1))
    gather_kv.far()
    kv_far = send(kv.at[c, replica(2)], kv.at[c, replica(2)], sibling)
    gather_wq.far()
    arrive(kv_far, kv.at[1 - c, replica(2)])
    project.add(replica(2))
    project.done()
    forward_attention(2, 2, M0)
    ag[M0].start()
    backward_attention(0, 0, 0)
    rows0 = RowSum(0)
    rows0.start()
    rs1 = ReduceScatter(1, normed_term(0))
    rs1.start()
    rows0.middle()
    ag[M0].middle()
    rs1.middle()
    ag[M0].finish()
    ag[M0].last()
    ysend[0] = output_projection(M0, gath[F0, c, 0])
    y_forward = send(ysend.at[0], yrecv.at[2], ydev(1))
    normed_grad = rs1.finish()
    result, gain_term0 = backward_result(0, normed_grad, rows0.finish())
    ysend[1] = result
    y_backward = send(ysend.at[1], yrecv.at[3], ydev(-1))

    arrive(y_forward, yrecv.at[2])

    @pl.when(s == 0)
    def _():
        gath[F1, c, 0] = fresh_rows(1)

    @pl.when(s != 0)
    def _():
        gath[F1, c, 0] = yrecv[2]

    ag[F1].start()
    arrive(y_backward, yrecv.at[3])
    grad_in[1] = jnp.where(s == SECTIONS - 1, loss_grad[1, 0], yrecv[3])
    rs2 = ReduceScatter(2, head_term(1))
    rs2.start()
    ag[F1].middle()
    rs2.middle()
    ag[F1].finish()
    ag[F1].last()
    project = Project((F1,), (3,))
    for owner in range(REPLICAS):
        project.add(owner)
    project.done()
    forward_attention(3, 3, M1)
    ag[M1].start()
    head_grad[1] = rs2.finish().astype(BF16)
    backward_attention(1, 1, 1)
    rows1 = RowSum(1)
    rows1.start()
    rs3 = ReduceScatter(3, normed_term(1))
    rs3.start()
    rows1.middle()
    ag[M1].middle()
    rs3.middle()
    ag[M1].finish()
    ag[M1].last()
    out_forward[0, 0] = output_projection(M1, gath[F1, c, 0])
    normed_grad = rs3.finish()
    result, gain_term1 = backward_result(1, normed_grad, rows1.finish())
    gain_all[0] = jnp.broadcast_to(gain_term0 + gain_term1, (8, BLK))
    gain_ids = [send(gain_all.at[0], gain_all.at[n], xdev(n)) for n in range(1, REPLICAS)]
    out_backward[0, 0] = result
    total = gain_all[0]
    for n in range(1, REPLICAS):
        arrive(gain_ids[n - 1], gain_all.at[n])
        total = total + gain_all[n]
    out_gain[...] = total[:1] * (1.0 / math.sqrt(TICKS * REPLICAS * ROWS))

    for copy in sends:
        copy.wait_send()

    @pl.when(s == 0)
    def _():
        for k in range(TICKS):
            for n in range(3):
                describe(fresh.at[k, 0], fr.at[k, d], fresh_ids[k][n], xdev(n + 1)).wait_send()


def local(*arguments):
    vmem = pl.BlockSpec(memory_space=pltpu.VMEM)
    anywhere = pl.BlockSpec(memory_space=pl.ANY)
    smem = pl.BlockSpec(memory_space=pltpu.SMEM)
    in_specs = [vmem] * 6 + [anywhere] * 4 + [smem, vmem, vmem, vmem]
    arguments = list(arguments)
    for n in (7, 8):
        arguments[n] = jnp.swapaxes(arguments[n], 1, 2)
    block = (ROWS, BLK)
    scratch = [
        pltpu.VMEM((MODEL_WIDTH, BLK), BF16),
        pltpu.VMEM((2, REPLICAS, HEAD, SHARD), BF16),
        pltpu.VMEM((MODEL_WIDTH, BLK), BF16),
        pltpu.VMEM((6, 2, RING) + block, BF16),
        pltpu.VMEM((2, RING, 16, BLK), F32),
        pltpu.VMEM((TICKS, REPLICAS) + block, BF16),
        pltpu.VMEM((4,) + block, BF16),
        pltpu.VMEM((2,) + block, BF16),
        pltpu.VMEM((TICKS,) + block, BF16),
        pltpu.VMEM((4, ROWS, ROWS), F32),
        pltpu.VMEM((4, 4, ROWS, HEAD), BF16),
        pltpu.VMEM((3 * ROWS, 512), F32),
        pltpu.VMEM((4, ROWS, HEAD), F32),
        pltpu.VMEM((4, RING) + block, BF16),
        pltpu.VMEM((4, RING) + block, BF16),
        pltpu.VMEM((4, RING) + block, BF16),
        pltpu.VMEM((4, 2) + block, BF16),
        pltpu.VMEM((4, 2, ROWS // 2, BLK), BF16),
        pltpu.VMEM((4, 4) + block, BF16),
        pltpu.VMEM((TICKS,) + block, BF16),
        pltpu.VMEM((TICKS, ROWS, 512), BF16),
        pltpu.VMEM((TICKS, 8, ROWS), F32),
        pltpu.VMEM((TICKS, 8, ROWS), F32),
        pltpu.VMEM((TICKS, RING, 8, ROWS), F32),
        pltpu.VMEM((REPLICAS, 8, BLK), F32),
        pltpu.SemaphoreType.DMA((SEMS,)),
        pltpu.SemaphoreType.DMA((SEMS,)),
        pltpu.SemaphoreType.DMA((4,)),
    ]
    return pl.pallas_call(
        kernel,
        out_shape=(
            jax.ShapeDtypeStruct((1, 1) + block, BF16),
            jax.ShapeDtypeStruct((1, 1) + block, BF16),
            jax.ShapeDtypeStruct((1, BLK), F32),
        ),
        in_specs=in_specs,
        out_specs=(vmem, vmem, vmem),
        scratch_shapes=scratch,
        compiler_params=pltpu.CompilerParams(
            collective_id=0, has_side_effects=True, vmem_limit_bytes=56 << 20
        ),
    )(*arguments)


def solution(mesh):
    return jax.shard_map(
        local,
        mesh=mesh,
        in_specs=(
            P("section", "dp", None, "tensor"),
            P(None, "dp", None, "tensor"),
            P(None, "section", "dp", None, "tensor"),
            P("section", "dp", None, "tensor"),
            P(None, "dp", None, "tensor"),
            P("section", "tensor"),
            P("section", "dp", "tensor"),
            P("section", "dp", "tensor"),
            P("section", "dp", "tensor"),
            P("section", "dp", "tensor"),
            P(),
            P(),
            P(None, "dp", None),
            P(None, "section", "dp", None),
        ),
        out_specs=(
            P("section", "dp", None, "tensor"),
            P("section", "dp", None, "tensor"),
            P("section", "tensor"),
        ),
        check_vma=False,
    )
```

```python
import math

import jax
import jax.numpy as jnp
from jax import lax
from jax.experimental import pallas as pl
from jax.experimental.pallas import tpu as pltpu
from jax.sharding import PartitionSpec as P

MODEL_WIDTH = 4096
HEAD = 128
TICKS = 2
ROWS = 128
BLK = 256
REPLICAS = 4
SECTIONS = 8
RING = 8
TENSOR = 16
SHARD = MODEL_WIDTH // REPLICAS
HALF = SHARD // 2
EPS = 1e-05
SCALE = HEAD ** (-0.5)
SEMS = 256
MESH = pl.DeviceIdType.MESH
F32 = jnp.float32
BF16 = jnp.bfloat16

S0, S1, F0, M0, F1, M1 = range(6)


def dot_nn(a, b):
    return lax.dot_general(a, b, (((1,), (0,)), ((), ())), preferred_element_type=F32)


def dot_nt(a, b):
    return lax.dot_general(a, b, (((1,), (1,)), ((), ())), preferred_element_type=F32)


def dot_tn(a, b):
    return lax.dot_general(a, b, (((0,), (0,)), ((), ())), preferred_element_type=F32)


def kernel(
    arrivals,
    fresh,
    stash,
    returning,
    loss_grad,
    gain,
    query_weight,
    key_weight,
    value_weight,
    w_out,
    plan,
    fresh_docs,
    arrival_docs,
    stash_docs,
    out_forward,
    out_backward,
    out_gain,
    wq,
    kv,
    ow,
    gath,
    gains,
    fr,
    yrecv,
    ysend,
    grad_in,
    masks,
    proj,
    proj_acc,
    inv_buf,
    part,
    part_sib,
    recv_sib,
    relay,
    relay_half,
    final,
    head_grad,
    grads,
    row_part,
    row_sib,
    row_all,
    gain_all,
    probs_buf,
    loss,
    term_own,
    term_x,
    term_z,
    ss,
    rs,
    ls,
):
    d = lax.axis_index("dp")
    s = lax.axis_index("section")
    t = lax.axis_index("tensor")
    z = t // 2
    c = t % 2

    def zdev(k):
        return (d, s, lax.rem(t + 2 * k + TENSOR, TENSOR))

    sibling = (d, s, t + 1 - 2 * c)

    def xdev(k):
        return (lax.rem(d + k + REPLICAS, REPLICAS), s, t)

    def ydev(k):
        return (d, lax.rem(s + k + SECTIONS, SECTIONS), t)

    sends = []
    counter = [0]

    def new_id():
        counter[0] += 1
        return counter[0] - 1

    def describe(src, dst, i, device):
        return pltpu.make_async_remote_copy(
            src_ref=src,
            dst_ref=dst,
            send_sem=ss.at[i],
            recv_sem=rs.at[i],
            device_id=device,
            device_id_type=MESH,
        )

    def send(src, dst, device, keep=True):
        i = new_id()
        copy = describe(src, dst, i, device)
        copy.start()
        if keep:
            sends.append(copy)
            return i
        return (i, copy)

    def arrive(i, dst):
        describe(dst, dst, i, sibling).wait_recv()

    own = pl.ds(pl.multiple_of(d * SHARD, SHARD), SHARD)
    load_ow = pltpu.make_async_copy(w_out.at[0], ow.at[own], ls.at[0])
    load_wq = pltpu.make_async_copy(query_weight.at[0], wq.at[own], ls.at[1])
    load_key = pltpu.make_async_copy(key_weight.at[0], kv.at[c, d, pl.ds(0, 64)], ls.at[2])
    load_value = pltpu.make_async_copy(value_weight.at[0], kv.at[c, d, pl.ds(64, 64)], ls.at[3])

    peers = [zdev(k) for k in range(1, RING)] + [sibling]
    peers += [xdev(k) for k in range(1, REPLICAS)] + [ydev(1), ydev(-1)]
    barrier = pltpu.get_barrier_semaphore()
    for peer in peers:
        pl.semaphore_signal(barrier, inc=1, device_id=peer, device_id_type=MESH)
    load_s0 = pltpu.make_async_copy(stash.at[0, 0, 0], gath.at[S0, c, 0], ls.at[4])
    load_s1 = pltpu.make_async_copy(stash.at[1, 0, 0], gath.at[S1, c, 0], ls.at[5])
    load_loss = pltpu.make_async_copy(loss_grad.at[pl.ds(0, TICKS), 0], loss, ls.at[6])
    load_fresh = pltpu.make_async_copy(
        fresh.at[pl.ds(0, TICKS), 0], fr.at[pl.ds(0, TICKS), d], ls.at[7]
    )
    for load in (load_s0, load_s1, load_loss, load_fresh, load_key, load_value, load_wq, load_ow):
        load.start()
    pl.semaphore_wait(barrier, len(peers))

    def replica(k):
        return lax.rem(d + k + REPLICAS, REPLICAS)

    def rows_at(buffer):
        def at(k, half):
            base = replica(k) * SHARD + half * HALF
            return buffer.at[pl.ds(pl.multiple_of(base, HALF), HALF)]

        return at

    def kv_at(k, half):
        return kv.at[c, replica(k), pl.ds(half * 64, 64)]

    class Gather:
        def __init__(self, at, first, second):
            self.at = at
            self.first = first
            self.second = second

        def start(self):
            at = self.at
            self.ids = [
                send(self.first, at(0, 0), xdev(1)),
                send(self.second, at(0, 1), xdev(-1)),
                send(self.second, at(0, 1), xdev(1)),
                send(self.first, at(0, 0), xdev(-1)),
            ]

        def forward(self):
            at = self.at
            arrive(self.ids[0], at(-1, 0))
            low = send(at(-1, 0), at(-1, 0), xdev(1))
            arrive(self.ids[1], at(1, 1))
            high = send(at(1, 1), at(1, 1), xdev(-1))
            self.ids += [low, high]

        def near(self):
            arrive(self.ids[2], self.at(-1, 1))
            arrive(self.ids[3], self.at(1, 0))

        def far(self):
            arrive(self.ids[4], self.at(2, 0))
            arrive(self.ids[5], self.at(2, 1))

    first, second = pl.ds(0, HALF), pl.ds(HALF, HALF)
    gather_ow = Gather(rows_at(ow), w_out.at[0, first], w_out.at[0, second])
    gather_wq = Gather(rows_at(wq), query_weight.at[0, first], query_weight.at[0, second])
    gather_kv = Gather(kv_at, key_weight.at[0], value_weight.at[0])

    gather_ow.start()

    y_forward = send(arrivals.at[0, 0], yrecv.at[0], ydev(1))
    y_backward = send(returning.at[0, 0], yrecv.at[1], ydev(-1))

    class AllGather:
        def __init__(self, buffer, half):
            self.b = buffer
            self.half = half

        def start(self):
            b = self.b
            src = b.at[c, 0]
            self.i3 = send(src, b.at[c, 3], zdev(2))
            self.i4 = send(src, b.at[c, 4], zdev(-2))
            self.i1 = send(src, b.at[c, 1], zdev(1))
            self.i2 = send(src, b.at[c, 2], zdev(-1))
            self.k0 = send(src, b.at[c, 0], sibling)

        def middle(self):
            b, h = self.b, self.half
            low, high = pl.ds(0, h), pl.ds(h, h)
            arrive(self.i3, b.at[c, 3])
            self.i5 = send(b.at[c, 3], b.at[c, 5], zdev(1))
            self.i7a = send(b.at[c, 3, low], b.at[c, 7, low], zdev(2))
            arrive(self.i4, b.at[c, 4])
            self.i6 = send(b.at[c, 4], b.at[c, 6], zdev(-1))
            self.i7b = send(b.at[c, 4, high], b.at[c, 7, high], zdev(-2))
            arrive(self.i1, b.at[c, 1])
            arrive(self.i2, b.at[c, 2])
            near = pl.ds(1, 4)
            self.k1 = send(b.at[c, near], b.at[c, near], sibling)

        def finish(self):
            b, h = self.b, self.half
            low, high = pl.ds(0, h), pl.ds(h, h)
            o = 1 - c
            arrive(self.i5, b.at[c, 5])
            arrive(self.i6, b.at[c, 6])
            arrive(self.i7a, b.at[c, 7, low])
            arrive(self.i7b, b.at[c, 7, high])
            away = pl.ds(5, 3)
            self.k2 = send(b.at[c, away], b.at[c, away], sibling)
            arrive(self.k0, b.at[o, 0])
            arrive(self.k1, b.at[o, pl.ds(1, 4)])

        def last(self):
            arrive(self.k2, self.b.at[1 - c, pl.ds(5, 3)])

    ag = [AllGather(gath.at[i], ROWS // 2) for i in range(6)]
    ag_gain = AllGather(gains, 8)

    load_s0.wait()
    load_s1.wait()
    gains[c, 0] = jnp.broadcast_to(gain[...], (16, BLK))
    ag_gain.start()
    ag[S0].start()
    ag[S1].start()

    fresh_ids = [[new_id() for _ in range(3)] for _ in range(TICKS)]

    @pl.when(s == 0)
    def _():
        for k in range(TICKS):
            for n in range(3):
                describe(fresh.at[k, 0], fr.at[k, d], fresh_ids[k][n], xdev(n + 1)).start()

    def fresh_rows(k):
        for n in range(3):
            source = lax.rem(d - n - 1 + REPLICAS, REPLICAS)
            arrive(fresh_ids[k][n], fr.at[k, source])
        total = jnp.zeros((ROWS, BLK), BF16)
        for p in range(REPLICAS):
            total = jnp.where(plan[k, d] == p, fr[k, p], total)
        return total

    def balanced(k):
        total = jnp.zeros((1, ROWS), jnp.int32)
        for p in range(REPLICAS):
            total = jnp.where(plan[k, d] == p, fresh_docs[k, pl.ds(p, 1), :], total)
        return total

    causal = lax.broadcasted_iota(jnp.int32, (ROWS, ROWS), 0) >= lax.broadcasted_iota(
        jnp.int32, (ROWS, ROWS), 1
    )

    def store_mask(index, docs):
        across = jnp.broadcast_to(docs.astype(F32), (ROWS, ROWS))
        allowed = jnp.logical_and(across == across.T, causal)
        masks[index] = jnp.where(allowed, 1.0, 0.0)

    store_mask(0, stash_docs[0, 0])
    store_mask(1, stash_docs[1, 0])
    first_docs = balanced(0)
    for k in range(TICKS):
        arrived = arrival_docs[jnp.maximum(s - k - 1, 0)]
        new = first_docs if k == 0 else jnp.where(s == 0, balanced(1), first_docs)
        store_mask(2 + k, jnp.where(s > k, arrived, new))

    load_loss.wait()
    load_fresh.wait()
    arrive(y_backward, yrecv.at[1])
    grad_in[0] = jnp.where(s == SECTIONS - 1, loss[0], yrecv[1])
    arrive(y_forward, yrecv.at[0])

    @pl.when(s == 0)
    def _():
        gath[F0, c, 0] = fresh_rows(0)

    @pl.when(s != 0)
    def _():
        gath[F0, c, 0] = yrecv[0]

    ag[F0].start()
    ag_gain.middle()
    ag[S0].middle()
    ag[S1].middle()

    def block_of(p, core):
        k = (p + 1) // 2
        off = k * (1 - 2 * (p % 2))
        return lax.rem(z + off + RING, RING) * 2 + core

    def slot_of(block):
        off = lax.rem(block // 2 - z + RING, RING)
        return 2 * off + (off // 4) * (15 - 4 * off)

    def rows_of(block):
        return pl.ds(pl.multiple_of(block * BLK, BLK), BLK)

    class ReduceScatter:
        def __init__(self, n, term):
            self.n = n
            self.term = term

        def fill(self, buffer, core, low, high):
            n, term = self.n, self.term

            def body(p, carry):
                buffer[n, p] = term(block_of(p, core)).astype(BF16)
                return carry

            lax.fori_loop(low, high, body, 0, unroll=high - low)

        def start(self, between=None):
            n = self.n
            away, near = pl.ds(5, 3), pl.ds(0, 5)
            self.fill(part_sib, 1 - c, 5, 8)
            self.k1 = send(part_sib.at[n, away], recv_sib.at[n, away], sibling)
            self.fill(part_sib, 1 - c, 0, 5)
            self.k0 = send(part_sib.at[n, near], recv_sib.at[n, near], sibling)
            self.fill(part, c, 5, 8)
            arrive(self.k1, recv_sib.at[n, away])
            for p in range(5, 8):
                self.add(p)
            low, high = pl.ds(0, ROWS // 2), pl.ds(ROWS // 2, ROWS // 2)
            self.ra = send(part.at[n, 5], relay.at[n, 0], zdev(-1))
            self.rb = send(part.at[n, 6], relay.at[n, 1], zdev(1))
            self.ha = send(part.at[n, 7, low], relay_half.at[n, 0], zdev(-2))
            self.hb = send(part.at[n, 7, high], relay_half.at[n, 1], zdev(2))
            if between is not None:
                between()
            self.fill(part, c, 0, 5)
            arrive(self.k0, recv_sib.at[n, near])
            for p in (1, 2):
                self.add(p)
            self.d0 = send(part.at[n, 1], final.at[n, 0], zdev(-1))
            self.d1 = send(part.at[n, 2], final.at[n, 1], zdev(1))

        def add(self, p):
            n = self.n
            part[n, p] = (part[n, p].astype(F32) + recv_sib[n, p].astype(F32)).astype(BF16)

        def middle(self):
            n = self.n
            h = ROWS // 2
            arrive(self.ra, relay.at[n, 0])
            arrive(self.ha, relay_half.at[n, 0])
            sum3 = part[n, 3].astype(F32) + recv_sib[n, 3].astype(F32) + relay[n, 0].astype(F32)
            part[n, 3, pl.ds(0, h)] = (sum3[:h] + relay_half[n, 0].astype(F32)).astype(BF16)
            part[n, 3, pl.ds(h, h)] = sum3[h:].astype(BF16)
            self.d2 = send(part.at[n, 3], final.at[n, 2], zdev(-2))
            arrive(self.rb, relay.at[n, 1])
            arrive(self.hb, relay_half.at[n, 1])
            sum4 = part[n, 4].astype(F32) + recv_sib[n, 4].astype(F32) + relay[n, 1].astype(F32)
            part[n, 4, pl.ds(0, h)] = sum4[:h].astype(BF16)
            part[n, 4, pl.ds(h, h)] = (sum4[h:] + relay_half[n, 1].astype(F32)).astype(BF16)
            self.d3 = send(part.at[n, 4], final.at[n, 3], zdev(2))

        def finish(self):
            n = self.n
            total = part[n, 0].astype(F32) + recv_sib[n, 0].astype(F32)
            for q, i in enumerate((self.d0, self.d1, self.d2, self.d3)):
                arrive(i, final.at[n, q])
                total = total + final[n, q].astype(F32)
            return total

    def head_term(k):
        def term(block):
            return dot_nt(grad_in[k], ow[rows_of(block), :])

        return term

    def kv_block(block):
        lanes = pl.ds(pl.multiple_of(lax.rem(block, 4) * BLK, BLK), BLK)
        return jnp.concatenate([kv[0, block // 4, :, lanes], kv[1, block // 4, :, lanes]], axis=0)

    def normed_term(k):
        def term(block):
            query_part = dot_nt(grads[k, :, pl.ds(0, BLK)], wq[rows_of(block), :])
            return query_part + dot_nn(grads[k, :, pl.ds(BLK, BLK)], kv_block(block))

        return term

    gather_ow.forward()
    gather_wq.start()
    for load in (load_key, load_value, load_wq, load_ow):
        load.wait()
    kv_own = send(kv.at[c, d], kv.at[c, d], sibling)
    ag[F0].middle()
    ag_gain.finish()
    ag[S0].finish()
    ag[S1].finish()
    ag[F0].finish()
    gather_ow.near()
    gather_kv.start()
    gather_wq.forward()
    gather_ow.far()
    rs0 = ReduceScatter(0, head_term(0))
    rs0.start()
    gather_kv.forward()
    rs0.middle()
    for index in (S0, S1, F0):
        ag[index].last()
    ag_gain.last()
    head_grad[0] = rs0.finish().astype(BF16)

    lane = lax.broadcasted_iota(jnp.int32, (ROWS, HEAD), 1)

    class Project:
        def __init__(self, indices, slots):
            self.indices = indices
            self.slots = slots
            count = len(indices)
            self.rows = pl.ds(0, count * ROWS)
            proj_acc[self.rows, :] = jnp.zeros((count * ROWS, 512), F32)
            self.squares = (jnp.zeros((ROWS, HEAD), F32),) * count

        def add(self, owner):
            rows = self.rows
            squares = list(self.squares)
            columns = []
            for q in range(4):
                block = owner * 4 + q
                p, core = slot_of(block), q % 2
                g = gains[core, p, pl.ds(0, 1), :]
                pieces = []
                for n, index in enumerate(self.indices):
                    h = gath[index, core, p].astype(F32)
                    sq = h * h
                    squares[n] = squares[n] + sq[:, :HEAD] + sq[:, HEAD:]
                    pieces.append((h * g).astype(BF16))
                columns.append(jnp.concatenate(pieces, axis=0))
            self.squares = squares
            lhs = jnp.concatenate(columns, axis=1)
            weight = wq[pl.ds(pl.multiple_of(owner * SHARD, SHARD), SHARD), :]
            proj_acc[rows, pl.ds(0, BLK)] += dot_nn(lhs, weight)
            both = jnp.concatenate([kv[0, owner], kv[1, owner]], axis=0)
            proj_acc[rows, pl.ds(BLK, BLK)] += dot_nt(lhs, both)

        def done(self):
            for n, slot in enumerate(self.slots):
                total = jnp.sum(self.squares[n], axis=-1, keepdims=True)
                inv = lax.rsqrt(total / MODEL_WIDTH + EPS)
                inv_buf[slot] = jnp.broadcast_to(inv, (ROWS, HEAD))
                acc = proj_acc[pl.ds(n * ROWS, ROWS), :] * inv
                low = acc[:, 256:384]
                high = acc[:, 384:512]
                key = jnp.where(lane < 64, low, pltpu.roll(high, 64, 1))
                value = jnp.where(lane < 64, pltpu.roll(low, 64, 1), high)
                proj[slot, 0] = acc[:, :128].astype(BF16)
                proj[slot, 1] = acc[:, 128:256].astype(BF16)
                proj[slot, 2] = key.astype(BF16)
                proj[slot, 3] = value.astype(BF16)

    def attention(slot, mask):
        q2 = jnp.concatenate([proj[slot, 0], proj[slot, 1]], axis=0)
        scores = dot_nt(q2, proj[slot, 2]) * SCALE
        allowed = jnp.concatenate([masks[mask], masks[mask]], axis=0) > 0.0
        raised = jnp.where(allowed, jnp.exp(scores), 0.0)
        return q2, raised / jnp.sum(raised, axis=-1, keepdims=True)

    def forward_attention(slot, mask, index):
        _, probs = attention(slot, mask)
        mixed = dot_nn(probs.astype(BF16), proj[slot, 3]).astype(BF16)
        gath[index, c, 0] = jnp.concatenate([mixed[:ROWS], mixed[ROWS:]], axis=1)

    def backward_attention(slot, k):
        q2 = jnp.concatenate([proj[slot, 0], proj[slot, 1]], axis=0)
        probs = probs_buf[...]
        key, value = proj[slot, 2], proj[slot, 3]
        hg = head_grad[k]
        hg2 = jnp.concatenate([hg[:, :HEAD], hg[:, HEAD:]], axis=0)
        prob_grad = dot_nt(hg2, value)
        inner = jnp.sum(probs * prob_grad, axis=-1, keepdims=True)
        score_grad = (probs * (prob_grad - inner) * SCALE).astype(BF16)
        query_grad = dot_nn(score_grad, key).astype(BF16).astype(F32)
        key_grad = dot_tn(score_grad, q2).astype(BF16).astype(F32)
        value_grad = dot_tn(probs.astype(BF16), hg2).astype(BF16).astype(F32)
        qf = q2.astype(F32)
        products = query_grad[:ROWS] * qf[:ROWS] + query_grad[ROWS:] * qf[ROWS:]
        products = products + key_grad * key.astype(F32) + value_grad * value.astype(F32)
        row = jnp.sum(products.T, axis=0, keepdims=True)
        row_part[k] = jnp.broadcast_to(row, (8, ROWS))
        low = jnp.where(lane < 64, key_grad, pltpu.roll(value_grad, 64, 1))
        high = jnp.where(lane < 64, pltpu.roll(key_grad, 64, 1), value_grad)
        grads[k] = jnp.concatenate(
            [query_grad[:ROWS], query_grad[ROWS:], low, high], axis=1
        ).astype(BF16)

    class RowSum:
        def __init__(self, k):
            self.k = k

        def start(self):
            self.i = send(row_part.at[self.k], row_sib.at[self.k], sibling)

        def middle(self):
            k = self.k
            arrive(self.i, row_sib.at[k])
            row_all[k, 0] = row_part[k] + row_sib[k]
            self.ids = [
                send(row_all.at[k, 0], row_all.at[k, n], zdev(n)) for n in range(1, RING)
            ]

        def finish(self):
            k = self.k
            total = row_all[k, 0]
            for n in range(1, RING):
                arrive(self.ids[n - 1], row_all.at[k, n])
                total = total + row_all[k, n]
            return jnp.broadcast_to(total[:1], (ROWS, ROWS)).T

    def backward_result(k, normed_grad, row):
        h = gath[(S0, S1)[k], c, 0].astype(F32)
        inv = inv_buf[k][:, :1]
        scaled = normed_grad * gain[...]
        factor = inv * inv * row[:, :1] * (1.0 / MODEL_WIDTH)
        result = grad_in[k].astype(F32) + inv * scaled - h * factor
        return result.astype(BF16), h * inv

    def output_projection(index, hidden):
        acc = hidden.astype(F32)
        for part_of in range(2):
            blocks = range(part_of * 8, part_of * 8 + 8)
            lhs = jnp.concatenate([gath[index, b % 2, slot_of(b)] for b in blocks], axis=1)
            acc = acc + dot_nn(lhs, ow[pl.ds(part_of * 8 * BLK, 8 * BLK), :])
        return acc.astype(BF16)

    project = Project((S0, S1, F0), (0, 1, 2))
    arrive(kv_own, kv.at[1 - c, d])
    project.add(replica(0))
    gather_kv.near()
    kv_ids = [send(kv.at[c, replica(k)], kv.at[c, replica(k)], sibling) for k in (-1, 1)]
    gather_wq.near()
    for i, k in zip(kv_ids, (-1, 1)):
        arrive(i, kv.at[1 - c, replica(k)])
    project.add(replica(-1))
    project.add(replica(1))
    gather_kv.far()
    kv_far = send(kv.at[c, replica(2)], kv.at[c, replica(2)], sibling)
    gather_wq.far()
    arrive(kv_far, kv.at[1 - c, replica(2)])
    project.add(replica(2))
    project.done()
    forward_attention(2, 2, M0)
    ag[M0].start()
    probs_buf[...] = attention(0, 0)[1]
    backward_attention(0, 0)
    rows0 = RowSum(0)
    rows0.start()
    rs1 = ReduceScatter(1, normed_term(0))
    rs1.start()
    rows0.middle()
    ag[M0].middle()
    rs1.middle()
    ag[M0].finish()
    ag[M0].last()
    ysend[0] = output_projection(M0, gath[F0, c, 0])
    y_forward = send(ysend.at[0], yrecv.at[2], ydev(1))
    probs_buf[...] = attention(1, 1)[1]
    normed_grad = rs1.finish()
    result, unit = backward_result(0, normed_grad, rows0.finish())
    ysend[1] = result
    y_backward = send(ysend.at[1], yrecv.at[3], ydev(-1))
    gain_all[0] = jnp.broadcast_to(jnp.sum(normed_grad * unit, axis=0, keepdims=True), (8, BLK))
    gain_ids = [send(gain_all.at[0], gain_all.at[n], xdev(n)) for n in range(1, REPLICAS)]

    arrive(y_forward, yrecv.at[2])

    @pl.when(s == 0)
    def _():
        gath[F1, c, 0] = fresh_rows(1)

    @pl.when(s != 0)
    def _():
        gath[F1, c, 0] = yrecv[2]

    ag[F1].start()
    arrive(y_backward, yrecv.at[3])
    grad_in[1] = jnp.where(s == SECTIONS - 1, loss[1], yrecv[3])
    rs2 = ReduceScatter(2, head_term(1))
    rs2.start()
    ag[F1].middle()
    rs2.middle()
    ag[F1].finish()
    ag[F1].last()
    project = Project((F1,), (3,))
    for owner in range(REPLICAS):
        project.add(owner)
    project.done()
    forward_attention(3, 3, M1)
    ag[M1].start()
    head_grad[1] = rs2.finish().astype(BF16)
    backward_attention(1, 1)
    rows1 = RowSum(1)
    rows1.start()
    rs3 = ReduceScatter(3, normed_term(1))
    rs3.start(ag[M1].middle)
    rows1.middle()
    inv1 = inv_buf[1][:, :1]
    for p in range(RING):
        piece = part[3, p].astype(F32)
        if p in (0, 3, 4):
            piece = piece + recv_sib[3, p].astype(F32)
        unit = gath[S1, c, p].astype(F32) * inv1
        term_own[p] = jnp.broadcast_to(jnp.sum(piece * unit, axis=0, keepdims=True), (8, BLK))
    term_ids = [send(term_own, term_x.at[n], xdev(n)) for n in range(1, REPLICAS)]
    rs3.middle()
    for n in range(1, REPLICAS):
        arrive(term_ids[n - 1], term_x.at[n])
    term_x[0] = term_own[...] + term_x[1] + term_x[2] + term_x[3]
    term_ids = []
    for p, off, back in ((1, -1, 2), (2, 1, 1), (3, -2, 4), (4, 2, 3), (5, -3, 6), (6, 3, 5), (7, 4, 7)):
        term_ids.append((send(term_x.at[0, p], term_z.at[back], zdev(off)), back))
    ag[M1].finish()
    ag[M1].last()
    out_forward[0, 0] = output_projection(M1, gath[F1, c, 0])
    normed_grad = rs3.finish()
    result, unit = backward_result(1, normed_grad, rows1.finish())
    out_backward[0, 0] = result
    total = gain_all[0] + term_x[0, 0]
    for n in range(1, REPLICAS):
        arrive(gain_ids[n - 1], gain_all.at[n])
        total = total + gain_all[n]
    for i, back in term_ids:
        arrive(i, term_z.at[back])
        total = total + term_z[back]
    out_gain[...] = total[:1] * (1.0 / math.sqrt(TICKS * REPLICAS * ROWS))

    for copy in sends:
        copy.wait_send()

    @pl.when(s == 0)
    def _():
        for k in range(TICKS):
            for n in range(3):
                describe(fresh.at[k, 0], fr.at[k, d], fresh_ids[k][n], xdev(n + 1)).wait_send()


def local(*arguments):
    vmem = pl.BlockSpec(memory_space=pltpu.VMEM)
    anywhere = pl.BlockSpec(memory_space=pl.ANY)
    smem = pl.BlockSpec(memory_space=pltpu.SMEM)
    in_specs = [anywhere] * 5 + [vmem] + [anywhere] * 4 + [smem, vmem, vmem, vmem]
    arguments = list(arguments)
    for n in (7, 8):
        arguments[n] = jnp.swapaxes(arguments[n], 1, 2)
    block = (ROWS, BLK)
    scratch = [
        pltpu.VMEM((MODEL_WIDTH, BLK), BF16),
        pltpu.VMEM((2, REPLICAS, HEAD, SHARD), BF16),
        pltpu.VMEM((MODEL_WIDTH, BLK), BF16),
        pltpu.VMEM((6, 2, RING) + block, BF16),
        pltpu.VMEM((2, RING, 16, BLK), F32),
        pltpu.VMEM((TICKS, REPLICAS) + block, BF16),
        pltpu.VMEM((4,) + block, BF16),
        pltpu.VMEM((2,) + block, BF16),
        pltpu.VMEM((TICKS,) + block, BF16),
        pltpu.VMEM((4, ROWS, ROWS), F32),
        pltpu.VMEM((4, 4, ROWS, HEAD), BF16),
        pltpu.VMEM((3 * ROWS, 512), F32),
        pltpu.VMEM((4, ROWS, HEAD), F32),
        pltpu.VMEM((4, RING) + block, BF16),
        pltpu.VMEM((4, RING) + block, BF16),
        pltpu.VMEM((4, RING) + block, BF16),
        pltpu.VMEM((4, 2) + block, BF16),
        pltpu.VMEM((4, 2, ROWS // 2, BLK), BF16),
        pltpu.VMEM((4, 4) + block, BF16),
        pltpu.VMEM((TICKS,) + block, BF16),
        pltpu.VMEM((TICKS, ROWS, 512), BF16),
        pltpu.VMEM((TICKS, 8, ROWS), F32),
        pltpu.VMEM((TICKS, 8, ROWS), F32),
        pltpu.VMEM((TICKS, RING, 8, ROWS), F32),
        pltpu.VMEM((REPLICAS, 8, BLK), F32),
        pltpu.VMEM((2 * ROWS, ROWS), F32),
        pltpu.VMEM((TICKS,) + block, BF16),
        pltpu.VMEM((RING, 8, BLK), F32),
        pltpu.VMEM((REPLICAS, RING, 8, BLK), F32),
        pltpu.VMEM((RING, 8, BLK), F32),
        pltpu.SemaphoreType.DMA((SEMS,)),
        pltpu.SemaphoreType.DMA((SEMS,)),
        pltpu.SemaphoreType.DMA((8,)),
    ]
    return pl.pallas_call(
        kernel,
        out_shape=(
            jax.ShapeDtypeStruct((1, 1) + block, BF16),
            jax.ShapeDtypeStruct((1, 1) + block, BF16),
            jax.ShapeDtypeStruct((1, BLK), F32),
        ),
        in_specs=in_specs,
        out_specs=(vmem, vmem, vmem),
        scratch_shapes=scratch,
        compiler_params=pltpu.CompilerParams(
            collective_id=0, has_side_effects=True, vmem_limit_bytes=56 << 20
        ),
    )(*arguments)


def solution(mesh):
    return jax.shard_map(
        local,
        mesh=mesh,
        in_specs=(
            P("section", "dp", None, "tensor"),
            P(None, "dp", None, "tensor"),
            P(None, "section", "dp", None, "tensor"),
            P("section", "dp", None, "tensor"),
            P(None, "dp", None, "tensor"),
            P("section", "tensor"),
            P("section", "dp", "tensor"),
            P("section", "dp", "tensor"),
            P("section", "dp", "tensor"),
            P("section", "dp", "tensor"),
            P(),
            P(),
            P(None, "dp", None),
            P(None, "section", "dp", None),
        ),
        out_specs=(
            P("section", "dp", None, "tensor"),
            P("section", "dp", None, "tensor"),
            P("section", "tensor"),
        ),
        check_vma=False,
    )
```

```python
import math

import jax
import jax.numpy as jnp
from jax import lax
from jax.experimental import pallas as pl
from jax.experimental.pallas import tpu as pltpu
from jax.sharding import PartitionSpec as P

MODEL_WIDTH = 4096
HEAD = 128
TICKS = 2
ROWS = 128
BLK = 256
REPLICAS = 4
SECTIONS = 8
RING = 8
TENSOR = 16
SHARD = MODEL_WIDTH // REPLICAS
HALF = SHARD // 2
EPS = 1e-05
SCALE = HEAD ** (-0.5)
SEMS = 256
MESH = pl.DeviceIdType.MESH
F32 = jnp.float32
BF16 = jnp.bfloat16

S0, S1, F0, M0, F1, M1 = range(6)


def dot_nn(a, b):
    return lax.dot_general(a, b, (((1,), (0,)), ((), ())), preferred_element_type=F32)


def dot_nt(a, b):
    return lax.dot_general(a, b, (((1,), (1,)), ((), ())), preferred_element_type=F32)


def dot_tn(a, b):
    return lax.dot_general(a, b, (((0,), (0,)), ((), ())), preferred_element_type=F32)


def kernel(
    arrivals,
    fresh,
    stash,
    returning,
    loss_grad,
    gain,
    query_weight,
    key_weight,
    value_weight,
    w_out,
    plan,
    fresh_docs,
    arrival_docs,
    stash_docs,
    out_forward,
    out_backward,
    out_gain,
    wq,
    kv,
    ow,
    gath,
    gains,
    fr,
    yrecv,
    ysend,
    grad_in,
    masks,
    proj,
    proj_acc,
    inv_buf,
    part,
    part_sib,
    recv_sib,
    relay,
    relay_half,
    final,
    head_grad,
    grads,
    row_part,
    row_sib,
    row_all,
    gain_all,
    probs_buf,
    loss,
    term_own,
    term_x,
    term_z,
    ss,
    rs,
    ls,
):
    d = lax.axis_index("dp")
    s = lax.axis_index("section")
    t = lax.axis_index("tensor")
    z = t // 2
    c = t % 2

    def zdev(k):
        return (d, s, lax.rem(t + 2 * k + TENSOR, TENSOR))

    sibling = (d, s, t + 1 - 2 * c)

    def xdev(k):
        return (lax.rem(d + k + REPLICAS, REPLICAS), s, t)

    def ydev(k):
        return (d, lax.rem(s + k + SECTIONS, SECTIONS), t)

    sends = []
    counter = [0]

    def new_id():
        counter[0] += 1
        return counter[0] - 1

    def describe(src, dst, i, device):
        return pltpu.make_async_remote_copy(
            src_ref=src,
            dst_ref=dst,
            send_sem=ss.at[i],
            recv_sem=rs.at[i],
            device_id=device,
            device_id_type=MESH,
        )

    def send(src, dst, device, keep=True):
        i = new_id()
        copy = describe(src, dst, i, device)
        copy.start()
        if keep:
            sends.append(copy)
            return i
        return (i, copy)

    def arrive(i, dst):
        describe(dst, dst, i, sibling).wait_recv()

    own = pl.ds(pl.multiple_of(d * SHARD, SHARD), SHARD)
    load_ow = pltpu.make_async_copy(w_out.at[0], ow.at[own], ls.at[0])
    load_wq = pltpu.make_async_copy(query_weight.at[0], wq.at[own], ls.at[1])
    load_key = pltpu.make_async_copy(key_weight.at[0], kv.at[c, d, pl.ds(0, 64)], ls.at[2])
    load_value = pltpu.make_async_copy(value_weight.at[0], kv.at[c, d, pl.ds(64, 64)], ls.at[3])

    peers = [zdev(k) for k in range(1, RING)] + [sibling]
    peers += [xdev(k) for k in range(1, REPLICAS)] + [ydev(1), ydev(-1)]
    barrier = pltpu.get_barrier_semaphore()
    for peer in peers:
        pl.semaphore_signal(barrier, inc=1, device_id=peer, device_id_type=MESH)
    load_s0 = pltpu.make_async_copy(stash.at[0, 0, 0], gath.at[S0, c, 0], ls.at[4])
    load_s1 = pltpu.make_async_copy(stash.at[1, 0, 0], gath.at[S1, c, 0], ls.at[5])
    load_loss = pltpu.make_async_copy(loss_grad.at[pl.ds(0, TICKS), 0], loss, ls.at[6])
    load_fresh = pltpu.make_async_copy(
        fresh.at[pl.ds(0, TICKS), 0], fr.at[pl.ds(0, TICKS), d], ls.at[7]
    )
    for load in (load_s0, load_s1, load_loss, load_fresh, load_key, load_value, load_wq, load_ow):
        load.start()
    pl.semaphore_wait(barrier, len(peers))

    def replica(k):
        return lax.rem(d + k + REPLICAS, REPLICAS)

    def rows_at(buffer):
        def at(k, half):
            base = replica(k) * SHARD + half * HALF
            return buffer.at[pl.ds(pl.multiple_of(base, HALF), HALF)]

        return at

    def kv_at(k, half):
        return kv.at[c, replica(k), pl.ds(half * 64, 64)]

    class Gather:
        def __init__(self, at, first, second):
            self.at = at
            self.first = first
            self.second = second

        def start(self):
            at = self.at
            self.ids = [
                send(self.first, at(0, 0), xdev(1)),
                send(self.second, at(0, 1), xdev(-1)),
                send(self.second, at(0, 1), xdev(1)),
                send(self.first, at(0, 0), xdev(-1)),
            ]

        def forward(self):
            at = self.at
            arrive(self.ids[0], at(-1, 0))
            low = send(at(-1, 0), at(-1, 0), xdev(1))
            arrive(self.ids[1], at(1, 1))
            high = send(at(1, 1), at(1, 1), xdev(-1))
            self.ids += [low, high]

        def near(self):
            arrive(self.ids[2], self.at(-1, 1))
            arrive(self.ids[3], self.at(1, 0))

        def far(self):
            arrive(self.ids[4], self.at(2, 0))
            arrive(self.ids[5], self.at(2, 1))

    first, second = pl.ds(0, HALF), pl.ds(HALF, HALF)
    gather_ow = Gather(rows_at(ow), w_out.at[0, first], w_out.at[0, second])
    gather_wq = Gather(rows_at(wq), query_weight.at[0, first], query_weight.at[0, second])
    gather_kv = Gather(kv_at, key_weight.at[0], value_weight.at[0])

    gather_ow.start()

    y_forward = send(arrivals.at[0, 0], yrecv.at[0], ydev(1))
    y_backward = send(returning.at[0, 0], yrecv.at[1], ydev(-1))

    class AllGather:
        def __init__(self, buffer, half):
            self.b = buffer
            self.half = half

        def start(self):
            b = self.b
            src = b.at[c, 0]
            self.i3 = send(src, b.at[c, 3], zdev(2))
            self.i4 = send(src, b.at[c, 4], zdev(-2))
            self.i1 = send(src, b.at[c, 1], zdev(1))
            self.i2 = send(src, b.at[c, 2], zdev(-1))
            self.k0 = send(src, b.at[c, 0], sibling)

        def middle(self):
            b, h = self.b, self.half
            low, high = pl.ds(0, h), pl.ds(h, h)
            arrive(self.i3, b.at[c, 3])
            self.i5 = send(b.at[c, 3], b.at[c, 5], zdev(1))
            self.i7a = send(b.at[c, 3, low], b.at[c, 7, low], zdev(2))
            arrive(self.i4, b.at[c, 4])
            self.i6 = send(b.at[c, 4], b.at[c, 6], zdev(-1))
            self.i7b = send(b.at[c, 4, high], b.at[c, 7, high], zdev(-2))
            arrive(self.i1, b.at[c, 1])
            arrive(self.i2, b.at[c, 2])
            near = pl.ds(1, 4)
            self.k1 = send(b.at[c, near], b.at[c, near], sibling)

        def finish(self):
            b, h = self.b, self.half
            low, high = pl.ds(0, h), pl.ds(h, h)
            o = 1 - c
            arrive(self.i5, b.at[c, 5])
            arrive(self.i6, b.at[c, 6])
            arrive(self.i7a, b.at[c, 7, low])
            arrive(self.i7b, b.at[c, 7, high])
            away = pl.ds(5, 3)
            self.k2 = send(b.at[c, away], b.at[c, away], sibling)
            arrive(self.k0, b.at[o, 0])
            arrive(self.k1, b.at[o, pl.ds(1, 4)])

        def last(self):
            arrive(self.k2, self.b.at[1 - c, pl.ds(5, 3)])

    ag = [AllGather(gath.at[i], ROWS // 2) for i in range(6)]
    ag_gain = AllGather(gains, 8)

    load_s0.wait()
    load_s1.wait()
    gains[c, 0] = jnp.broadcast_to(gain[...], (16, BLK))
    ag_gain.start()
    ag[S0].start()
    ag[S1].start()

    fresh_ids = [[new_id() for _ in range(3)] for _ in range(TICKS)]

    @pl.when(s == 0)
    def _():
        for k in range(TICKS):
            for n in range(3):
                describe(fresh.at[k, 0], fr.at[k, d], fresh_ids[k][n], xdev(n + 1)).start()

    def fresh_rows(k):
        for n in range(3):
            source = lax.rem(d - n - 1 + REPLICAS, REPLICAS)
            arrive(fresh_ids[k][n], fr.at[k, source])
        total = jnp.zeros((ROWS, BLK), BF16)
        for p in range(REPLICAS):
            total = jnp.where(plan[k, d] == p, fr[k, p], total)
        return total

    def balanced(k):
        total = jnp.zeros((1, ROWS), jnp.int32)
        for p in range(REPLICAS):
            total = jnp.where(plan[k, d] == p, fresh_docs[k, pl.ds(p, 1), :], total)
        return total

    causal = lax.broadcasted_iota(jnp.int32, (ROWS, ROWS), 0) >= lax.broadcasted_iota(
        jnp.int32, (ROWS, ROWS), 1
    )

    def store_mask(index, docs):
        across = jnp.broadcast_to(docs.astype(F32), (ROWS, ROWS))
        allowed = jnp.logical_and(across == across.T, causal)
        masks[index] = jnp.where(allowed, 1.0, 0.0)

    store_mask(0, stash_docs[0, 0])
    store_mask(1, stash_docs[1, 0])
    first_docs = balanced(0)
    for k in range(TICKS):
        arrived = arrival_docs[jnp.maximum(s - k - 1, 0)]
        new = first_docs if k == 0 else jnp.where(s == 0, balanced(1), first_docs)
        store_mask(2 + k, jnp.where(s > k, arrived, new))

    load_loss.wait()
    load_fresh.wait()
    arrive(y_backward, yrecv.at[1])
    grad_in[0] = jnp.where(s == SECTIONS - 1, loss[0], yrecv[1])
    arrive(y_forward, yrecv.at[0])

    @pl.when(s == 0)
    def _():
        gath[F0, c, 0] = fresh_rows(0)

    @pl.when(s != 0)
    def _():
        gath[F0, c, 0] = yrecv[0]

    ag[F0].start()
    ag_gain.middle()
    ag[S0].middle()
    ag[S1].middle()

    def block_of(p, core):
        k = (p + 1) // 2
        off = k * (1 - 2 * (p % 2))
        return lax.rem(z + off + RING, RING) * 2 + core

    def slot_of(block):
        off = lax.rem(block // 2 - z + RING, RING)
        return 2 * off + (off // 4) * (15 - 4 * off)

    def rows_of(block):
        return pl.ds(pl.multiple_of(block * BLK, BLK), BLK)

    class ReduceScatter:
        def __init__(self, n, term):
            self.n = n
            self.term = term

        def fill(self, buffer, core, low, high):
            n, term = self.n, self.term

            def body(p, carry):
                buffer[n, p] = term(block_of(p, core)).astype(BF16)
                return carry

            lax.fori_loop(low, high, body, 0, unroll=high - low)

        def start(self, between=None):
            n = self.n
            away, near = pl.ds(5, 3), pl.ds(0, 5)
            self.fill(part_sib, 1 - c, 5, 8)
            self.k1 = send(part_sib.at[n, away], recv_sib.at[n, away], sibling)
            self.fill(part_sib, 1 - c, 0, 5)
            self.k0 = send(part_sib.at[n, near], recv_sib.at[n, near], sibling)
            self.fill(part, c, 5, 8)
            arrive(self.k1, recv_sib.at[n, away])
            for p in range(5, 8):
                self.add(p)
            low, high = pl.ds(0, ROWS // 2), pl.ds(ROWS // 2, ROWS // 2)
            self.ra = send(part.at[n, 5], relay.at[n, 0], zdev(-1))
            self.rb = send(part.at[n, 6], relay.at[n, 1], zdev(1))
            self.ha = send(part.at[n, 7, low], relay_half.at[n, 0], zdev(-2))
            self.hb = send(part.at[n, 7, high], relay_half.at[n, 1], zdev(2))
            if between is not None:
                between()
            self.fill(part, c, 0, 5)
            arrive(self.k0, recv_sib.at[n, near])
            for p in (1, 2):
                self.add(p)
            self.d0 = send(part.at[n, 1], final.at[n, 0], zdev(-1))
            self.d1 = send(part.at[n, 2], final.at[n, 1], zdev(1))

        def add(self, p):
            n = self.n
            part[n, p] = (part[n, p].astype(F32) + recv_sib[n, p].astype(F32)).astype(BF16)

        def middle(self):
            n = self.n
            h = ROWS // 2
            arrive(self.ra, relay.at[n, 0])
            arrive(self.ha, relay_half.at[n, 0])
            sum3 = part[n, 3].astype(F32) + recv_sib[n, 3].astype(F32) + relay[n, 0].astype(F32)
            part[n, 3, pl.ds(0, h)] = (sum3[:h] + relay_half[n, 0].astype(F32)).astype(BF16)
            part[n, 3, pl.ds(h, h)] = sum3[h:].astype(BF16)
            self.d2 = send(part.at[n, 3], final.at[n, 2], zdev(-2))
            arrive(self.rb, relay.at[n, 1])
            arrive(self.hb, relay_half.at[n, 1])
            sum4 = part[n, 4].astype(F32) + recv_sib[n, 4].astype(F32) + relay[n, 1].astype(F32)
            part[n, 4, pl.ds(0, h)] = sum4[:h].astype(BF16)
            part[n, 4, pl.ds(h, h)] = (sum4[h:] + relay_half[n, 1].astype(F32)).astype(BF16)
            self.d3 = send(part.at[n, 4], final.at[n, 3], zdev(2))

        def finish(self):
            n = self.n
            total = part[n, 0].astype(F32) + recv_sib[n, 0].astype(F32)
            for q, i in enumerate((self.d0, self.d1, self.d2, self.d3)):
                arrive(i, final.at[n, q])
                total = total + final[n, q].astype(F32)
            return total

    def head_term(k):
        def term(block):
            return dot_nt(grad_in[k], ow[rows_of(block), :])

        return term

    def kv_block(block):
        lanes = pl.ds(pl.multiple_of(lax.rem(block, 4) * BLK, BLK), BLK)
        return jnp.concatenate([kv[0, block // 4, :, lanes], kv[1, block // 4, :, lanes]], axis=0)

    def normed_term(k):
        def term(block):
            query_part = dot_nt(grads[k, :, pl.ds(0, BLK)], wq[rows_of(block), :])
            return query_part + dot_nn(grads[k, :, pl.ds(BLK, BLK)], kv_block(block))

        return term

    gather_ow.forward()
    gather_wq.start()
    for load in (load_key, load_value, load_wq, load_ow):
        load.wait()
    kv_own = send(kv.at[c, d], kv.at[c, d], sibling)
    ag[F0].middle()
    ag_gain.finish()
    ag[S0].finish()
    ag[S1].finish()
    ag[F0].finish()
    gather_ow.near()
    gather_kv.start()
    gather_wq.forward()
    gather_ow.far()
    rs0 = ReduceScatter(0, head_term(0))
    rs0.start()
    gather_kv.forward()
    rs0.middle()
    for index in (S0, S1, F0):
        ag[index].last()
    ag_gain.last()
    head_grad[0] = rs0.finish().astype(BF16)

    lane = lax.broadcasted_iota(jnp.int32, (ROWS, HEAD), 1)

    class Project:
        def __init__(self, indices, slots):
            self.indices = indices
            self.slots = slots
            count = len(indices)
            self.rows = pl.ds(0, count * ROWS)
            proj_acc[self.rows, :] = jnp.zeros((count * ROWS, 512), F32)
            self.squares = (jnp.zeros((ROWS, HEAD), F32),) * count

        def add(self, owner):
            rows = self.rows
            squares = list(self.squares)
            columns = []
            for q in range(4):
                block = owner * 4 + q
                p, core = slot_of(block), q % 2
                g = gains[core, p, pl.ds(0, 1), :]
                pieces = []
                for n, index in enumerate(self.indices):
                    h = gath[index, core, p].astype(F32)
                    sq = h * h
                    squares[n] = squares[n] + sq[:, :HEAD] + sq[:, HEAD:]
                    pieces.append((h * g).astype(BF16))
                columns.append(jnp.concatenate(pieces, axis=0))
            self.squares = squares
            lhs = jnp.concatenate(columns, axis=1)
            weight = wq[pl.ds(pl.multiple_of(owner * SHARD, SHARD), SHARD), :]
            proj_acc[rows, pl.ds(0, BLK)] += dot_nn(lhs, weight)
            both = jnp.concatenate([kv[0, owner], kv[1, owner]], axis=0)
            proj_acc[rows, pl.ds(BLK, BLK)] += dot_nt(lhs, both)

        def done(self):
            for n, slot in enumerate(self.slots):
                total = jnp.sum(self.squares[n], axis=-1, keepdims=True)
                inv = lax.rsqrt(total / MODEL_WIDTH + EPS)
                inv_buf[slot] = jnp.broadcast_to(inv, (ROWS, HEAD))
                acc = proj_acc[pl.ds(n * ROWS, ROWS), :] * inv
                low = acc[:, 256:384]
                high = acc[:, 384:512]
                key = jnp.where(lane < 64, low, pltpu.roll(high, 64, 1))
                value = jnp.where(lane < 64, pltpu.roll(low, 64, 1), high)
                proj[slot, 0] = acc[:, :128].astype(BF16)
                proj[slot, 1] = acc[:, 128:256].astype(BF16)
                proj[slot, 2] = key.astype(BF16)
                proj[slot, 3] = value.astype(BF16)

    def attention(slot, mask):
        q2 = jnp.concatenate([proj[slot, 0], proj[slot, 1]], axis=0)
        scores = dot_nt(q2, proj[slot, 2]) * SCALE
        allowed = jnp.concatenate([masks[mask], masks[mask]], axis=0) > 0.0
        raised = jnp.where(allowed, jnp.exp(scores), 0.0)
        return q2, raised / jnp.sum(raised, axis=-1, keepdims=True)

    def forward_attention(slot, mask, index):
        _, probs = attention(slot, mask)
        mixed = dot_nn(probs.astype(BF16), proj[slot, 3]).astype(BF16)
        gath[index, c, 0] = jnp.concatenate([mixed[:ROWS], mixed[ROWS:]], axis=1)

    def backward_attention(slot, k):
        q2 = jnp.concatenate([proj[slot, 0], proj[slot, 1]], axis=0)
        probs = probs_buf[...]
        key, value = proj[slot, 2], proj[slot, 3]
        hg = head_grad[k]
        hg2 = jnp.concatenate([hg[:, :HEAD], hg[:, HEAD:]], axis=0)
        prob_grad = dot_nt(hg2, value)
        inner = jnp.sum(probs * prob_grad, axis=-1, keepdims=True)
        score_grad = (probs * (prob_grad - inner) * SCALE).astype(BF16)
        query_grad = dot_nn(score_grad, key).astype(BF16).astype(F32)
        key_grad = dot_tn(score_grad, q2).astype(BF16).astype(F32)
        value_grad = dot_tn(probs.astype(BF16), hg2).astype(BF16).astype(F32)
        qf = q2.astype(F32)
        products = query_grad[:ROWS] * qf[:ROWS] + query_grad[ROWS:] * qf[ROWS:]
        products = products + key_grad * key.astype(F32) + value_grad * value.astype(F32)
        row = jnp.sum(products.T, axis=0, keepdims=True)
        row_part[k] = jnp.broadcast_to(row, (8, ROWS))
        low = jnp.where(lane < 64, key_grad, pltpu.roll(value_grad, 64, 1))
        high = jnp.where(lane < 64, pltpu.roll(key_grad, 64, 1), value_grad)
        grads[k] = jnp.concatenate(
            [query_grad[:ROWS], query_grad[ROWS:], low, high], axis=1
        ).astype(BF16)

    class RowSum:
        def __init__(self, k):
            self.k = k

        def start(self):
            self.i = send(row_part.at[self.k], row_sib.at[self.k], sibling)

        def middle(self):
            k = self.k
            arrive(self.i, row_sib.at[k])
            row_all[k, 0] = row_part[k] + row_sib[k]
            self.ids = [
                send(row_all.at[k, 0], row_all.at[k, n], zdev(n)) for n in range(1, RING)
            ]

        def finish(self):
            k = self.k
            total = row_all[k, 0]
            for n in range(1, RING):
                arrive(self.ids[n - 1], row_all.at[k, n])
                total = total + row_all[k, n]
            return jnp.broadcast_to(total[:1], (ROWS, ROWS)).T

    def backward_result(k, normed_grad, row):
        h = gath[(S0, S1)[k], c, 0].astype(F32)
        inv = inv_buf[k][:, :1]
        scaled = normed_grad * gain[...]
        factor = inv * inv * row[:, :1] * (1.0 / MODEL_WIDTH)
        result = grad_in[k].astype(F32) + inv * scaled - h * factor
        return result.astype(BF16), h * inv

    def output_projection(index, hidden):
        acc = hidden.astype(F32)
        for part_of in range(2):
            blocks = range(part_of * 8, part_of * 8 + 8)
            lhs = jnp.concatenate([gath[index, b % 2, slot_of(b)] for b in blocks], axis=1)
            acc = acc + dot_nn(lhs, ow[pl.ds(part_of * 8 * BLK, 8 * BLK), :])
        return acc.astype(BF16)

    project = Project((S0, S1, F0), (0, 1, 2))
    arrive(kv_own, kv.at[1 - c, d])
    project.add(replica(0))
    gather_kv.near()
    kv_ids = [send(kv.at[c, replica(k)], kv.at[c, replica(k)], sibling) for k in (-1, 1)]
    gather_wq.near()
    for i, k in zip(kv_ids, (-1, 1)):
        arrive(i, kv.at[1 - c, replica(k)])
    project.add(replica(-1))
    project.add(replica(1))
    gather_kv.far()
    kv_far = send(kv.at[c, replica(2)], kv.at[c, replica(2)], sibling)
    gather_wq.far()
    arrive(kv_far, kv.at[1 - c, replica(2)])
    project.add(replica(2))
    project.done()
    forward_attention(2, 2, M0)
    ag[M0].start()
    probs_buf[...] = attention(0, 0)[1]
    backward_attention(0, 0)
    rows0 = RowSum(0)
    rows0.start()
    rs1 = ReduceScatter(1, normed_term(0))
    rs1.start()
    rows0.middle()
    ag[M0].middle()
    rs1.middle()
    ag[M0].finish()
    ag[M0].last()
    ysend[0] = output_projection(M0, gath[F0, c, 0])
    y_forward = send(ysend.at[0], yrecv.at[2], ydev(1))
    normed_grad = rs1.finish()
    result, unit = backward_result(0, normed_grad, rows0.finish())
    ysend[1] = result
    y_backward = send(ysend.at[1], yrecv.at[3], ydev(-1))
    gain_all[0] = jnp.broadcast_to(jnp.sum(normed_grad * unit, axis=0, keepdims=True), (8, BLK))
    gain_ids = [send(gain_all.at[0], gain_all.at[n], xdev(n)) for n in range(1, REPLICAS)]

    arrive(y_forward, yrecv.at[2])

    @pl.when(s == 0)
    def _():
        gath[F1, c, 0] = fresh_rows(1)

    @pl.when(s != 0)
    def _():
        gath[F1, c, 0] = yrecv[2]

    ag[F1].start()
    probs_buf[...] = attention(1, 1)[1]
    arrive(y_backward, yrecv.at[3])
    grad_in[1] = jnp.where(s == SECTIONS - 1, loss[1], yrecv[3])
    rs2 = ReduceScatter(2, head_term(1))
    rs2.start(ag[F1].middle)
    rs2.middle()
    ag[F1].finish()
    ag[F1].last()
    project = Project((F1,), (3,))
    for owner in range(REPLICAS):
        project.add(owner)
    project.done()
    forward_attention(3, 3, M1)
    ag[M1].start()
    head_grad[1] = rs2.finish().astype(BF16)
    backward_attention(1, 1)
    rows1 = RowSum(1)
    rows1.start()
    rs3 = ReduceScatter(3, normed_term(1))
    rs3.start(ag[M1].middle)
    rows1.middle()
    inv1 = inv_buf[1][:, :1]
    for p in range(RING):
        piece = part[3, p].astype(F32)
        if p in (0, 3, 4):
            piece = piece + recv_sib[3, p].astype(F32)
        unit = gath[S1, c, p].astype(F32) * inv1
        term_own[p] = jnp.broadcast_to(jnp.sum(piece * unit, axis=0, keepdims=True), (8, BLK))
    term_ids = [send(term_own, term_x.at[n], xdev(n)) for n in range(1, REPLICAS)]
    rs3.middle()
    for n in range(1, REPLICAS):
        arrive(term_ids[n - 1], term_x.at[n])
    term_x[0] = term_own[...] + term_x[1] + term_x[2] + term_x[3]
    term_ids = []
    for p, off, back in ((1, -1, 2), (2, 1, 1), (3, -2, 4), (4, 2, 3), (5, -3, 6), (6, 3, 5), (7, 4, 7)):
        term_ids.append((send(term_x.at[0, p], term_z.at[back], zdev(off)), back))
    ag[M1].finish()
    ag[M1].last()
    out_forward[0, 0] = output_projection(M1, gath[F1, c, 0])
    normed_grad = rs3.finish()
    result, unit = backward_result(1, normed_grad, rows1.finish())
    out_backward[0, 0] = result
    total = gain_all[0] + term_x[0, 0]
    for n in range(1, REPLICAS):
        arrive(gain_ids[n - 1], gain_all.at[n])
        total = total + gain_all[n]
    for i, back in term_ids:
        arrive(i, term_z.at[back])
        total = total + term_z[back]
    out_gain[...] = total[:1] * (1.0 / math.sqrt(TICKS * REPLICAS * ROWS))

    for copy in sends:
        copy.wait_send()

    @pl.when(s == 0)
    def _():
        for k in range(TICKS):
            for n in range(3):
                describe(fresh.at[k, 0], fr.at[k, d], fresh_ids[k][n], xdev(n + 1)).wait_send()


def local(*arguments):
    vmem = pl.BlockSpec(memory_space=pltpu.VMEM)
    anywhere = pl.BlockSpec(memory_space=pl.ANY)
    smem = pl.BlockSpec(memory_space=pltpu.SMEM)
    in_specs = [anywhere] * 5 + [vmem] + [anywhere] * 4 + [smem, vmem, vmem, vmem]
    arguments = list(arguments)
    for n in (7, 8):
        arguments[n] = jnp.swapaxes(arguments[n], 1, 2)
    block = (ROWS, BLK)
    scratch = [
        pltpu.VMEM((MODEL_WIDTH, BLK), BF16),
        pltpu.VMEM((2, REPLICAS, HEAD, SHARD), BF16),
        pltpu.VMEM((MODEL_WIDTH, BLK), BF16),
        pltpu.VMEM((6, 2, RING) + block, BF16),
        pltpu.VMEM((2, RING, 16, BLK), F32),
        pltpu.VMEM((TICKS, REPLICAS) + block, BF16),
        pltpu.VMEM((4,) + block, BF16),
        pltpu.VMEM((2,) + block, BF16),
        pltpu.VMEM((TICKS,) + block, BF16),
        pltpu.VMEM((4, ROWS, ROWS), F32),
        pltpu.VMEM((4, 4, ROWS, HEAD), BF16),
        pltpu.VMEM((3 * ROWS, 512), F32),
        pltpu.VMEM((4, ROWS, HEAD), F32),
        pltpu.VMEM((4, RING) + block, BF16),
        pltpu.VMEM((4, RING) + block, BF16),
        pltpu.VMEM((4, RING) + block, BF16),
        pltpu.VMEM((4, 2) + block, BF16),
        pltpu.VMEM((4, 2, ROWS // 2, BLK), BF16),
        pltpu.VMEM((4, 4) + block, BF16),
        pltpu.VMEM((TICKS,) + block, BF16),
        pltpu.VMEM((TICKS, ROWS, 512), BF16),
        pltpu.VMEM((TICKS, 8, ROWS), F32),
        pltpu.VMEM((TICKS, 8, ROWS), F32),
        pltpu.VMEM((TICKS, RING, 8, ROWS), F32),
        pltpu.VMEM((REPLICAS, 8, BLK), F32),
        pltpu.VMEM((2 * ROWS, ROWS), F32),
        pltpu.VMEM((TICKS,) + block, BF16),
        pltpu.VMEM((RING, 8, BLK), F32),
        pltpu.VMEM((REPLICAS, RING, 8, BLK), F32),
        pltpu.VMEM((RING, 8, BLK), F32),
        pltpu.SemaphoreType.DMA((SEMS,)),
        pltpu.SemaphoreType.DMA((SEMS,)),
        pltpu.SemaphoreType.DMA((8,)),
    ]
    return pl.pallas_call(
        kernel,
        out_shape=(
            jax.ShapeDtypeStruct((1, 1) + block, BF16),
            jax.ShapeDtypeStruct((1, 1) + block, BF16),
            jax.ShapeDtypeStruct((1, BLK), F32),
        ),
        in_specs=in_specs,
        out_specs=(vmem, vmem, vmem),
        scratch_shapes=scratch,
        compiler_params=pltpu.CompilerParams(
            collective_id=0, has_side_effects=True, vmem_limit_bytes=56 << 20
        ),
    )(*arguments)


def solution(mesh):
    return jax.shard_map(
        local,
        mesh=mesh,
        in_specs=(
            P("section", "dp", None, "tensor"),
            P(None, "dp", None, "tensor"),
            P(None, "section", "dp", None, "tensor"),
            P("section", "dp", None, "tensor"),
            P(None, "dp", None, "tensor"),
            P("section", "tensor"),
            P("section", "dp", "tensor"),
            P("section", "dp", "tensor"),
            P("section", "dp", "tensor"),
            P("section", "dp", "tensor"),
            P(),
            P(),
            P(None, "dp", None),
            P(None, "section", "dp", None),
        ),
        out_specs=(
            P("section", "dp", None, "tensor"),
            P("section", "dp", None, "tensor"),
            P("section", "tensor"),
        ),
        check_vma=False,
    )
```
